32 devices in a mesh: ctx: 8 (over z, x), head: 4 (over y, core).
Axes of the slice: x: 2, y: 2, z: 4, core: 2. Of those that a mesh axis runs over, the one named last changes fastest.
Arguments:
- token_keys: bfloat16 [8, 2048, 128], P(None, ('ctx', 'head')), may hold values from -4.5 to 4.5
- token_values: bfloat16 [8, 2048, 128], P(None, ('ctx', 'head')), may hold values from -6 to 6
- queries: bfloat16 [8, 2048, 8, 128], P(None, ('ctx', 'head')), may hold values from -16 to 16
- out_grad: bfloat16 [8, 2048, 8, 128], P(None, ('ctx', 'head')), may hold values from -6 to 6
- slot_ids: int32 [8, 2048], P('head'), may hold values from 0 to 511, as said below
Outputs:
- attended: bfloat16 [8, 2048, 8, 128], P(None, ('ctx', 'head'))
- key_grad: float32 [8, 2048, 128], P(None, ('ctx', 'head'))
- value_grad: float32 [8, 2048, 128], P(None, ('ctx', 'head'))
The draws below stay inside these ranges and needn't reach their ends.
Inputs may be any that keep to these rules, and one draw needn't show every extreme that they name: `slot_ids`: in each head's row slot numbers never fall; each of the 512 slots holds 1 to 16 consecutive tokens; slots k * 64 to (k + 1) * 64 - 1 all begin among tokens k * 256 to (k + 1) * 256 - 1; every such block of tokens holds a slot of exactly 16 tokens.
All inputs are finite; a program needn't handle non-finite values.
Results may differ from the reference program's by a relative error of at most 0.012.
The reference program's roundings to bfloat16 on the way (of `slot_pairs`, `weights_low`, `dscores` and `slot_grads`) count: a program that leaves them out, or rounds other values in their place, can miss the bound.
Values may be sent and summed in bfloat16 or wider, within the bound.
A program may use at most 64 MiB of HBM per device.

```python
import math
import jax
import jax.numpy as jnp
from jax import lax

HEAD_DIM = 128
GROUP = 8
KV_HEADS = 8
RATIO = 4
RUN_MAX = 16
TOK_DEV = 256
CTX = 2048
SLOTS = 512
SLOT_DEV = 64
QUERIES = 2048
STRIDE = 1


def draw_token_keys(key, part):
    base_key = jax.random.fold_in(key, 11)
    shape_all = (KV_HEADS, CTX, HEAD_DIM)
    drawn = jnp.clip(jax.random.normal(base_key, shape_all, jnp.float32), -4.0, 4.0)
    return drawn.astype(jnp.bfloat16)


def draw_queries(key, part):
    base_key = jax.random.fold_in(key, 13)
    shape_all = (KV_HEADS, QUERIES, GROUP, HEAD_DIM)
    drawn = jnp.clip(4.0 * jax.random.normal(base_key, shape_all, jnp.float32), -16.0, 16.0)
    return drawn.astype(jnp.bfloat16)


def draw_slot_ids(key, part):
    blocks = CTX // TOK_DEV
    per_block = SLOT_DEV
    block_index = jnp.arange(blocks, dtype=jnp.int32)
    offsets = jax.random.randint(jax.random.fold_in(key, 21), (KV_HEADS, blocks), 1, 4).astype(jnp.int32)
    offsets = jnp.where(block_index[None, :] == 0, 0, offsets)
    next_off = jnp.concatenate([offsets[:, 1:], jnp.zeros((KV_HEADS, 1), jnp.int32)], axis=1)
    group_at = jax.random.randint(jax.random.fold_in(key, 22), (KV_HEADS, blocks, 1), 0, per_block - 5).astype(jnp.int32)
    amounts = jax.random.randint(jax.random.fold_in(key, 23), (KV_HEADS, blocks, per_block // 2), -3, 4).astype(jnp.int32)
    slot_pos = jnp.arange(per_block, dtype=jnp.int32)[None, None, :]
    in_group = (slot_pos >= group_at) & (slot_pos < group_at + 5)
    group_len = jnp.where(slot_pos == group_at, RUN_MAX, 1)
    rank = jnp.where(slot_pos < group_at, slot_pos, slot_pos - 5)
    pair_index = jnp.clip(rank // 2, 0, per_block // 2 - 1)
    amount = jnp.take_along_axis(amounts, pair_index, axis=2)
    pair_len = RATIO + jnp.where(rank % 2 == 0, amount, -amount)
    last_len = (RATIO + next_off - offsets)[:, :, None]
    lengths = jnp.where(in_group, group_len, jnp.where(slot_pos == per_block - 1, last_len, pair_len)).astype(jnp.int32)
    starts = offsets[:, :, None] + jnp.cumsum(lengths, axis=2) - lengths
    token_pos = jnp.arange(TOK_DEV, dtype=jnp.int32)
    counted = jnp.sum((starts[:, :, None, :] <= token_pos[None, None, :, None]).astype(jnp.int32), axis=3)
    ids = block_index[None, :, None] * per_block + counted - 1
    return ids.reshape(KV_HEADS, CTX).astype(jnp.int32)


def levels(own_key, shape, cuts, smallest, high):
    loudness, own = 1.0, jax.random.fold_in(own_key, 6)
    for axis_at, shards_of in cuts:
        draws = jnp.exp(jax.random.uniform(jax.random.fold_in(own, axis_at), (shards_of,), jnp.float32, smallest / len(cuts), high / len(cuts)))
        loudness = loudness * jnp.repeat(draws, shape[axis_at] // shards_of).reshape([-1 if axis == axis_at else 1 for axis in range(len(shape))])
    return loudness


def gaussian(rng, extent, width, bound, cuts=(), kind=jnp.bfloat16):
    entries = width * jax.random.normal(rng, extent, jnp.float32)
    if cuts:
        entries = entries * levels(rng, extent, cuts, -0.22, 0.18)
    return jnp.clip(entries, -bound, bound).astype(kind)


def setup_inputs(seed: int = 0) -> dict:
    streams_of = jax.random.split(jax.random.key(seed), 6)
    return {
        "token_keys": draw_token_keys(jax.random.fold_in(streams_of[5], 71), 0),
        "token_values": gaussian(streams_of[1], (KV_HEADS, CTX, HEAD_DIM), 1.0, 6.0, ((1, 32),)),
        "queries": draw_queries(jax.random.fold_in(streams_of[5], 71), 0),
        "out_grad": gaussian(streams_of[3], (KV_HEADS, QUERIES, GROUP, HEAD_DIM), 1.0, 6.0, ((1, 32),)),
        "slot_ids": draw_slot_ids(jax.random.fold_in(streams_of[5], 71), 0),
    }


neg_big = -1e+30

def slot_table(id_row):
    slot_edges = jnp.searchsorted(id_row, jnp.arange(SLOTS + 1, dtype=jnp.int32), side='left').astype(jnp.int32)
    return (slot_edges[:-1], slot_edges[1:] - slot_edges[:-1])

def one_head(inputs):
    head_keys, head_values, head_queries, head_grads, id_row = inputs
    slot_start, slot_len = slot_table(id_row)
    lengths = slot_len.astype(jnp.float32)[:, None]
    pair_data = jnp.concatenate([head_keys, head_values], axis=1).astype(jnp.float32)
    slot_sums = jax.ops.segment_sum(pair_data, id_row, num_segments=SLOTS)
    slot_pairs = (slot_sums / lengths).astype(jnp.bfloat16)
    slot_keys = slot_pairs[:, :HEAD_DIM]
    slot_vals = slot_pairs[:, HEAD_DIM:]
    score_scale = 1.0 / math.sqrt(HEAD_DIM)
    total_rows = QUERIES * GROUP
    block_rows = math.gcd(2048, total_rows)
    query_rows = head_queries.reshape(total_rows // block_rows, block_rows, HEAD_DIM)
    grad_rows = head_grads.reshape(total_rows // block_rows, block_rows, HEAD_DIM)
    positions = jnp.arange(QUERIES, dtype=jnp.int32) * STRIDE + STRIDE - 1
    positions = jnp.repeat(positions, GROUP).reshape(total_rows // block_rows, block_rows)

    def scan_step(totals, block_in):
        q_block, g_block, p_block = block_in
        scores = jnp.dot(q_block, slot_keys.T, preferred_element_type=jnp.float32) * score_scale
        visible = slot_start[None, :] <= p_block[:, None]
        row_top = lax.optimization_barrier(jnp.max(jnp.where(visible, scores, neg_big), axis=1, keepdims=True))
        raw_weights = jnp.where(visible, jnp.exp(scores - row_top), 0.0)
        weights = raw_weights / lax.optimization_barrier(jnp.sum(raw_weights, axis=1, keepdims=True))
        weights_low = weights.astype(jnp.bfloat16)
        attended = jnp.dot(weights_low, slot_vals, preferred_element_type=jnp.float32).astype(jnp.bfloat16)
        row_dot = lax.optimization_barrier(jnp.sum(g_block.astype(jnp.float32) * attended.astype(jnp.float32), axis=1, keepdims=True))
        weight_grads = jnp.dot(g_block, slot_vals.T, preferred_element_type=jnp.float32)
        dscores = (weights * (weight_grads - row_dot)).astype(jnp.bfloat16)
        value_grads = jnp.dot(weights_low.T, g_block, preferred_element_type=jnp.float32)
        key_grads = jnp.dot(dscores.T, q_block, preferred_element_type=jnp.float32) * score_scale
        return ((totals[0] + key_grads, totals[1] + value_grads), attended)
    zeros_init = jnp.zeros((SLOTS, HEAD_DIM), jnp.float32)
    (key_grads, value_grads), attended = lax.scan(scan_step, (zeros_init, zeros_init), (query_rows, grad_rows, positions))
    slot_grads = jnp.concatenate([key_grads, value_grads], axis=1).astype(jnp.bfloat16)
    token_grads = slot_grads[id_row].astype(jnp.float32) / lengths[id_row]
    return (attended.reshape(QUERIES, GROUP, HEAD_DIM), token_grads[:, :HEAD_DIM], token_grads[:, HEAD_DIM:])

def reference(token_keys, token_values, queries, out_grad, slot_ids):
    attended, key_grad, value_grad = lax.map(one_head, (token_keys, token_values, queries, out_grad, slot_ids))
    return (attended, key_grad, value_grad)
```

```python
import functools
import math

import jax
import jax.numpy as jnp
from jax import lax
from jax.experimental import pallas as pl
from jax.experimental.pallas import tpu as pltpu
from jax.sharding import PartitionSpec as P

RATIO = 4
EDGE = 16
LANES = 128
MESH = pl.DeviceIdType.MESH
neg_big = -1e30
bf, f32 = jnp.bfloat16, jnp.float32


def dot_nt(a, b):
    return lax.dot_general(a, b, (((1,), (1,)), ((), ())), preferred_element_type=f32)


def dot_tn(a, b):
    return lax.dot_general(a, b, (((0,), (0,)), ((), ())), preferred_element_type=f32)


def dot_nn(a, b):
    return lax.dot_general(a, b, (((1,), (0,)), ((), ())), preferred_element_type=f32)


def kernel(
    dims,
    q_ref, g_ref, k_ref, v_ref, id_ref,
    out_ref, rt, rx,
    idv, idb, thr, qg, tok, ext, kv, att, part, red, zout, zin, acc, tg, tgx,
    here, loc, tok_s, tok_r, ext_s, ext_r, id_s, id_r, sw_s, sw_r,
    kz_s, kz_r, kp_s, kp_r, pt_s, pt_r, zs_s, zs_r, at_s, at_r, tg_s, tg_r, tx_s, tx_r,
):
    nc, nx, nh, hpd, T, R, S, D = dims
    ny, nz = nh // 2, nc // nx
    plane = nx * ny
    TB = T * nh
    NS = nc * S
    group = R // T
    scale = 1.0 / math.sqrt(D)
    ctx = lax.axis_index("ctx")
    j = lax.axis_index("head")
    y, c = j // 2, lax.rem(j, 2)
    peer = y * 2 + 1 - c
    z, x = ctx // nx, lax.rem(ctx, nx)
    spot = x * ny + y

    def remote(src, dst, ssem, rsem, to_ctx, to_head):
        return pltpu.make_async_remote_copy(
            src_ref=src, dst_ref=dst, send_sem=ssem, recv_sem=rsem,
            device_id=(to_ctx, to_head), device_id_type=MESH,
        )

    def arrived(ref, sem):
        remote(ref, ref, sem, sem, ctx, peer).wait_recv()

    def sent(ref, sem):
        remote(ref, ref, sem, sem, ctx, peer).wait_send()

    def by_layers(fn):
        for n in range(1, nz + 1):
            @pl.when(z == n - 1)
            def _():
                fn(n)

    def heads(ref, owner):
        return ref.at[pl.ds(owner * hpd, hpd)]

    def in_plane(fn):
        @pl.loop(1, plane)
        def _(i):
            to = lax.rem(spot + i, plane)
            fn(to, to // ny, lax.rem(to, ny))

    ext[...] = jnp.zeros_like(ext)
    rx[...] = jnp.zeros_like(rx)

    get_ids = pltpu.make_async_copy(id_ref, idv, loc.at[0])
    get_ids.start()
    own_rows = []
    for yy in range(ny):
        own_rows.append(pltpu.make_async_copy(heads(q_ref, yy * 2 + c), qg.at[0, yy, 0], loc.at[1 + yy]))
        own_rows.append(pltpu.make_async_copy(heads(g_ref, yy * 2 + c), qg.at[0, yy, 1], loc.at[1 + yy]))

    barrier = pltpu.get_barrier_semaphore()

    def greet(to_ctx, to_head):
        pl.semaphore_signal(barrier, inc=1, device_id=(to_ctx, to_head), device_id_type=MESH)

    @pl.loop(1, nh)
    def _(i):
        greet(ctx, lax.rem(j + i, nh))

    @pl.loop(1, nx)
    def _(i):
        @pl.loop(0, ny)
        def _(yy):
            greet(z * nx + lax.rem(x + i, nx), yy * 2 + c)

    @pl.loop(z + 1, nz)
    def _(to):
        greet(to * nx + x, j)

    @pl.when(ctx < nc - 1)
    def _():
        greet(ctx + 1, 0)

    for cp in own_rows:
        cp.start()

    follows = (j == 0) & (ctx > 0)
    pl.semaphore_wait(barrier, nh - 1 + (nx - 1) * ny + z + jnp.where(follows, nh, 0))

    @pl.loop(0, z)
    def _(to):
        pl.semaphore_signal(here.at[z], inc=1, device_id=(to * nx + x, j), device_id_type=MESH)

    own_tok = [
        pltpu.make_async_copy(heads(k_ref, j), tok.at[0, :, j], loc.at[1 + ny]),
        pltpu.make_async_copy(heads(v_ref, j), tok.at[1, :, j], loc.at[1 + ny]),
    ]
    for cp in own_tok:
        cp.start()

    @pl.loop(1, nh)
    def _(i):
        to = lax.rem(j + i, nh)
        remote(heads(k_ref, to), tok.at[0, :, j], tok_s, tok_r.at[j], ctx, to).start()
        remote(heads(v_ref, to), tok.at[1, :, j], tok_s, tok_r.at[j], ctx, to).start()

    @pl.when(follows)
    def _():
        @pl.loop(0, nh)
        def _(to):
            for which, src in ((0, k_ref), (1, v_ref)):
                remote(
                    src.at[pl.ds(to * hpd, hpd), pl.ds(0, EDGE)], ext.at[which, :, pl.ds(0, EDGE)],
                    ext_s, ext_r, ctx - 1, to,
                ).start()

    get_ids.wait()
    idb[y] = idv[:, pl.ds(pl.multiple_of(ctx * TB, LANES), TB)] - ctx * S

    @pl.loop(1, ny)
    def _(i):
        remote(idb.at[y], idb.at[y], id_s, id_r.at[y], ctx, lax.rem(y + i, ny) * 2 + c).start()

    @pl.loop(0, ny)
    def _(i):
        yy = lax.rem(y + i, ny)
        remote(heads(q_ref, yy * 2 + 1 - c), qg.at[1, yy, 0], sw_s, sw_r.at[yy], ctx, peer).start()
        remote(heads(g_ref, yy * 2 + 1 - c), qg.at[1, yy, 1], sw_s, sw_r.at[yy], ctx, peer).start()

    next_at = pl.multiple_of(jnp.minimum(ctx + 1, nc - 1) * TB, LANES)

    def hot(h):
        main_ids = idv[h:h + 1, pl.ds(pl.multiple_of(ctx * TB, LANES), TB)] - ctx * S
        edge_ids = jnp.where(ctx < nc - 1, idv[h:h + 1, pl.ds(next_at, LANES)] - ctx * S, -1)
        main = lax.broadcasted_iota(jnp.int32, (S, TB), 0) == main_ids
        edge = lax.broadcasted_iota(jnp.int32, (S, LANES), 0) == edge_ids
        main, edge = main.astype(f32), edge.astype(f32)
        count = jnp.sum(main, axis=1, keepdims=True) + jnp.sum(edge, axis=1, keepdims=True)
        return main.astype(bf), edge.astype(bf), count

    @pl.loop(1, nh)
    def _(i):
        arrived(tok.at[:, :, lax.rem(j + i, nh)], tok_r.at[lax.rem(j + i, nh)])

    own = tok.at[:, :, j]
    pltpu.make_async_copy(own, own, loc.at[1 + ny]).wait()

    @pl.when(ctx < nc - 1)
    def _():
        arrived(ext.at[:, :, pl.ds(0, EDGE)], ext_r)

    for h in range(hpd):
        main, edge, count = hot(h)
        for which in range(2):
            total = dot_nn(main, tok[which, h].reshape(TB, D)) + dot_nn(edge, ext[which, h])
            kv[y, h, x, z, which] = (total / count).astype(bf)

    def spread(h, zs):
        blk = kv.at[y, h, x, zs]

        def give(to, to_x, to_y):
            remote(blk, blk, kp_s.at[to], kp_r.at[spot, h], z * nx + to_x, to_y * 2 + c).start()

        in_plane(give)

    for h in range(hpd):
        spread(h, z)

    @pl.loop(z + 1, nz)
    def _(to):
        pl.semaphore_wait(here.at[to], 1)
        for h in range(hpd):
            blk = kv.at[y, h, x, z]
            remote(blk, blk, kz_s, kz_r.at[z, h], to * nx + x, j).start()

    @pl.loop(z + 1, nz)
    def _(zs):
        for yy in range(ny):
            for h in range(hpd):
                for xs in range(nx):
                    kv[yy, h, xs, zs] = jnp.zeros((2, S, D), bf)

    @pl.loop(1, ny)
    def _(i):
        yy = lax.rem(y + i, ny)
        arrived(idb.at[yy], id_r.at[yy])

    for t in range(2):
        core = c if t == 0 else 1 - c
        token = lax.broadcasted_iota(jnp.int32, (TB, R), 0) - (y * 2 + core) * T
        first = lax.broadcasted_iota(jnp.int32, (TB, R), 1) - token * group
        pick = ((first >= 0) & (first < group)).astype(f32).astype(bf)
        for yy in range(ny):
            for h in range(hpd):
                ids = idb[yy, h:h + 1].astype(f32).astype(bf)
                row = dot_nn(jnp.broadcast_to(ids, (16, TB)), pick)
                thr[yy, h, t] = row[:1].astype(jnp.int32)

    for h in range(hpd):
        @pl.loop(0, z)
        def _(i):
            zs = z - 1 - i
            arrived(kv.at[y, h, x, zs], kz_r.at[zs, h])
            spread(h, zs)

    def reduce_plane(h):
        in_plane(lambda frm, fx, fy: by_layers(
            lambda n: arrived(red.at[frm, h, pl.ds(0, n)], pt_r.at[frm, h])
        ))

        def total(zb):
            out = part[y, h, x, zb].astype(f32)
            for i in range(1, plane):
                out += red[lax.rem(spot + i, plane), h, zb].astype(f32)
            return out

        @pl.loop(0, z)
        def _(zb):
            zout[h, zb] = total(zb).astype(bf)
            remote(zout.at[h, zb], zin.at[z, h], zs_s, zs_r.at[z, h], zb * nx + x, j).start()

        acc[h] = total(z)

    @pl.loop(0, hpd * ny)
    def _(u):
        h, k = u // ny, lax.rem(u, ny)
        yy = lax.rem(y + k, ny)

        @pl.when(h == 0)
        def _():
            pltpu.make_async_copy(qg.at[0, yy], qg.at[0, yy], loc.at[1 + yy]).wait()
            arrived(qg.at[1, yy], sw_r.at[yy])

        @pl.loop(0, nx)
        def _(i):
            xs = lax.rem(x + i, nx)

            @pl.when((i > 0) | (k > 0))
            def _():
                by_layers(lambda n: arrived(kv.at[yy, h, xs, pl.ds(0, n)], kp_r.at[xs * ny + yy, h]))

        keys = kv[yy, h, :, :, 0].reshape(NS, D)
        vals = kv[yy, h, :, :, 1].reshape(NS, D)
        key_sum = val_sum = None
        for t in range(2):
            rows, grads = qg[t, yy, 0, h], qg[t, yy, 1, h]
            bar = thr[yy, h, t]
            raw_scores = dot_nt(keys, rows).reshape(nx, nz, S, R)
            slot = lax.broadcasted_iota(jnp.int32, (S, R), 0)
            scores = jnp.concatenate([
                jnp.where(slot <= bar - (zb * nx + xb - ctx) * S, raw_scores[xb, zb], neg_big)
                for xb in range(nx) for zb in range(nz)
            ], axis=0)
            top = jnp.max(scores, axis=0, keepdims=True)
            raw = jnp.exp2((scores - top) * (scale * math.log2(math.e)))
            weights = raw * (1.0 / jnp.sum(raw, axis=0, keepdims=True))
            low = weights.astype(bf)
            seen = dot_tn(vals, low).astype(bf).astype(f32)
            grads_t = grads.astype(f32).T
            row_dot = jnp.sum(grads_t * seen, axis=0, keepdims=True)
            seen_rows = seen.T.astype(bf)
            if t == 0:
                out_ref[(yy * 2 + c) * hpd + h] = seen_rows
            else:
                att[yy, h] = seen_rows
            slope = (weights * (dot_nt(vals, grads) - row_dot)).astype(bf)
            val_grad = dot_nn(low, grads)
            key_grad = dot_nn(slope, rows)
            key_sum = key_grad if key_sum is None else key_sum + key_grad
            val_sum = val_grad if val_sum is None else val_sum + val_grad
        part[yy, h, :, :, :, :D] = (key_sum * scale).astype(bf).reshape(nx, nz, S, D)
        part[yy, h, :, :, :, D:] = val_sum.astype(bf).reshape(nx, nz, S, D)

        @pl.loop(0, nx)
        def _(i):
            xs = lax.rem(x + i, nx)

            @pl.when((i > 0) | (k > 0))
            def _():
                by_layers(lambda n: remote(
                    part.at[yy, h, xs, pl.ds(0, n)], red.at[spot, h, pl.ds(0, n)],
                    pt_s.at[xs * ny + yy], pt_r.at[spot, h], z * nx + xs, yy * 2 + c,
                ).start())

        remote(att.at[yy, h], out_ref.at[(yy * 2 + c) * hpd + h], at_s, at_r, ctx, peer).start()

        @pl.when((k == 0) & (h > 0))
        def _():
            reduce_plane(h - 1)

    reduce_plane(hpd - 1)

    for h in range(hpd):
        @pl.loop(z + 1, nz)
        def _(frm):
            arrived(zin.at[frm, h], zs_r.at[frm, h])
            acc[h] += zin[frm, h].astype(f32)

        main, edge, count = hot(h)
        unit = (acc[h].astype(bf).astype(f32) / count).astype(bf)
        spread_rows = dot_tn(main, unit).astype(bf)
        for to in range(nh):
            tg[to, h] = spread_rows[to * T:(to + 1) * T]
        tgx[h] = dot_tn(edge, unit)[:EDGE].astype(bf)

    @pl.loop(1, nh)
    def _(i):
        to = lax.rem(j + i, nh)
        remote(tg.at[to], heads(rt, j), tg_s, tg_r.at[j], ctx, to).start()

    @pl.when(ctx < nc - 1)
    def _():
        remote(tgx, heads(rx, j), tx_s, tx_r, ctx + 1, 0).start()

    rt[pl.ds(j * hpd, hpd)] = tg[j]

    sent(tok.at[:, :, pl.ds(0, nh - 1)], tok_s)

    @pl.when(follows)
    def _():
        sent(tok.at[:, :, :, pl.ds(0, EDGE)], ext_s)

    sent(idb.at[pl.ds(0, ny - 1)], id_s)
    sent(qg.at[1], sw_s)
    sent(att, at_s)
    arrived(att, at_r)
    for n in range(1, nz):
        @pl.when(z == nz - 1 - n)
        def _():
            sent(kv.at[y, :, x, pl.ds(0, n)], kz_s)

        @pl.when(z == n)
        def _():
            sent(zout.at[:, pl.ds(0, n)], zs_s)

    def plane_sent(to, to_x, to_y):
        def fn(n):
            sent(kv.at[y, :, x, pl.ds(0, n)], kp_s.at[to])
            sent(part.at[to_y, :, to_x, pl.ds(0, n)], pt_s.at[to])

        by_layers(fn)

    in_plane(plane_sent)

    @pl.loop(1, nh)
    def _(i):
        frm = lax.rem(j + i, nh)
        arrived(heads(rt, frm), tg_r.at[frm])

    @pl.when(follows)
    def _():
        arrived(rx, tx_r)

    sent(tg.at[pl.ds(0, nh - 1)], tg_s)

    @pl.when(ctx < nc - 1)
    def _():
        sent(tgx, tx_s)


def hand_over(a_ref, t_ref, x_ref, a_out, k_out, v_out, kbuf, vbuf, sem):
    D = k_out.shape[-1]
    whole = pltpu.make_async_copy(a_ref, a_out, sem.at[0])
    whole.start()
    copies = [whole]
    for i, (buf, out) in enumerate(((kbuf, k_out), (vbuf, v_out))):
        cols = slice(i * D, (i + 1) * D)
        buf[...] = t_ref[:, :, cols].astype(f32)
        buf[:, :EDGE] += x_ref[:, :, cols].astype(f32)
        copies.append(pltpu.make_async_copy(buf, out, sem.at[1 + i]))
        copies[-1].start()
    for cp in copies:
        cp.wait()


def per_device(nc, nh, token_keys, token_values, queries, out_grad, slot_ids):
    heads_all, T, D = token_keys.shape
    group = queries.shape[2]
    hpd, context = slot_ids.shape
    R = queries.shape[1] * group
    TB = T * nh
    S = TB // RATIO
    ny = nh // 2
    nx = 2 ** ((nc.bit_length() - 1) // 2)
    nz = nc // nx
    plane = nx * ny
    dma = pltpu.SemaphoreType.DMA
    anywhere = pl.BlockSpec(memory_space=pl.ANY)
    vmem = pl.BlockSpec(memory_space=pltpu.VMEM)
    results = pl.pallas_call(
        functools.partial(kernel, (nc, nx, nh, hpd, T, R, S, D)),
        out_shape=(
            pltpu.VMEM((heads_all, R, D), bf),
            pltpu.VMEM((heads_all, T, 2 * D), bf),
            pltpu.VMEM((heads_all, EDGE, 2 * D), bf),
        ),
        in_specs=[anywhere] * 5,
        out_specs=(vmem, vmem, vmem),
        scratch_shapes=[
            pltpu.VMEM((hpd, context), jnp.int32),
            pltpu.VMEM((ny, hpd, TB), jnp.int32),
            pltpu.VMEM((ny, hpd, 2, 1, R), jnp.int32),
            pltpu.VMEM((2, ny, 2, hpd, R, D), bf),
            pltpu.VMEM((2, hpd, nh, T, D), bf),
            pltpu.VMEM((2, hpd, LANES, D), bf),
            pltpu.VMEM((ny, hpd, nx, nz, 2, S, D), bf),
            pltpu.VMEM((ny, hpd, R, D), bf),
            pltpu.VMEM((ny, hpd, nx, nz, S, 2 * D), bf),
            pltpu.VMEM((plane, hpd, nz, S, 2 * D), bf),
            pltpu.VMEM((hpd, nz, S, 2 * D), bf),
            pltpu.VMEM((nz, hpd, S, 2 * D), bf),
            pltpu.VMEM((hpd, S, 2 * D), f32),
            pltpu.VMEM((nh, hpd, T, 2 * D), bf),
            pltpu.VMEM((hpd, EDGE, 2 * D), bf),
            pltpu.SemaphoreType.REGULAR((nz,)), dma((2 + ny,)),
            dma(()), dma((nh,)), dma(()), dma(()), dma(()), dma((ny,)), dma(()), dma((ny,)),
            dma(()), dma((nz, hpd)), dma((plane,)), dma((plane, hpd)), dma((plane,)), dma((plane, hpd)),
            dma(()), dma((nz, hpd)), dma(()), dma(()), dma(()), dma((nh,)), dma(()), dma(()),
        ],
        compiler_params=pltpu.CompilerParams(
            collective_id=0, has_side_effects=True, vmem_limit_bytes=48 << 20
        ),
    )(
        queries.reshape(heads_all, R, D), out_grad.reshape(heads_all, R, D),
        token_keys, token_values, slot_ids,
    )
    attended, grads, edges = [pltpu.with_memory_space_constraint(r, pltpu.VMEM) for r in results]
    attended, key_grad, value_grad = pl.pallas_call(
        hand_over,
        out_shape=(
            jax.ShapeDtypeStruct((heads_all, R, D), bf),
            jax.ShapeDtypeStruct((heads_all, T, D), f32),
            jax.ShapeDtypeStruct((heads_all, T, D), f32),
        ),
        in_specs=[vmem] * 3,
        out_specs=(anywhere,) * 3,
        scratch_shapes=[
            pltpu.VMEM((heads_all, T, D), f32), pltpu.VMEM((heads_all, T, D), f32), dma((3,)),
        ],
    )(attended, grads, edges)
    return attended.reshape(queries.shape), key_grad, value_grad


def solution(mesh):
    nc, nh = mesh.shape["ctx"], mesh.shape["head"]
    rows = P(None, ("ctx", "head"), None)
    grouped = P(None, ("ctx", "head"), None, None)
    return jax.shard_map(
        functools.partial(per_device, nc, nh),
        mesh=mesh,
        in_specs=(rows, rows, grouped, grouped, P("head", None)),
        out_specs=(grouped, rows, rows),
        check_vma=False,
    )
```

```python
import functools
import math

import jax
import jax.numpy as jnp
from jax import lax
from jax.experimental import pallas as pl
from jax.experimental.pallas import tpu as pltpu
from jax.sharding import PartitionSpec as P

RATIO = 4
EDGE = 16
LANES = 128
MESH = pl.DeviceIdType.MESH
neg_big = -1e30
bf, f32 = jnp.bfloat16, jnp.float32


def dot_nt(a, b):
    return lax.dot_general(a, b, (((1,), (1,)), ((), ())), preferred_element_type=f32)


def dot_tn(a, b):
    return lax.dot_general(a, b, (((0,), (0,)), ((), ())), preferred_element_type=f32)


def dot_nn(a, b):
    return lax.dot_general(a, b, (((1,), (0,)), ((), ())), preferred_element_type=f32)


def kernel(
    dims,
    q_ref, g_ref, k_ref, v_ref, id_ref,
    out_ref, rt, rx,
    idv, idb, thr, mains, edges, counts, qg, tok, ext, kv, att, part, red, zout, zin, far, fout, fin, acc, tg, tgx,
    here, loc, tok_s, tok_r, ext_s, ext_r, id_s, id_r, sw_s, sw_r,
    kz_s, kz_r, kp_s, kp_r, kd_s, kd_r, pt_s, pt_r, zs_s, zs_r, fz_s, fz_r, fp_s, fp_r, at_s, at_r, tg_s, tg_r, tx_s, tx_r,
):
    nc, nx, nh, hpd, T, R, S, D = dims
    ny, nz = nh // 2, nc // nx
    plane = nx * ny
    TB = T * nh
    NS = nc * S
    group = R // T
    scale = 1.0 / math.sqrt(D)
    ctx = lax.axis_index("ctx")
    j = lax.axis_index("head")
    y, c = j // 2, lax.rem(j, 2)
    peer = y * 2 + 1 - c
    z, x = ctx // nx, lax.rem(ctx, nx)
    spot = x * ny + y

    def remote(src, dst, ssem, rsem, to_ctx, to_head):
        return pltpu.make_async_remote_copy(
            src_ref=src, dst_ref=dst, send_sem=ssem, recv_sem=rsem,
            device_id=(to_ctx, to_head), device_id_type=MESH,
        )

    def arrived(ref, sem):
        remote(ref, ref, sem, sem, ctx, peer).wait_recv()

    def sent(ref, sem):
        remote(ref, ref, sem, sem, ctx, peer).wait_send()

    def by_layers(fn):
        for n in range(1, nz + 1):
            @pl.when(z == n - 1)
            def _():
                fn(n)

    def heads(ref, owner):
        return ref.at[pl.ds(owner * hpd, hpd)]

    def near(fn):
        @pl.loop(1, nx)
        def _(i):
            fn(lax.rem(x + i, nx), y)

        @pl.loop(1, ny)
        def _(i):
            fn(x, lax.rem(y + i, ny))

    def apart(fn):
        @pl.loop(1, nx)
        def _(i):
            @pl.loop(1, ny)
            def _(e):
                fn(lax.rem(x + i, nx), lax.rem(y + e, ny))

    def in_plane(fn):
        near(fn)
        apart(fn)

    ext[...] = jnp.zeros_like(ext)
    rx[...] = jnp.zeros_like(rx)

    get_ids = pltpu.make_async_copy(id_ref, idv, loc.at[0])
    get_ids.start()
    own_rows = []
    for yy in range(ny):
        own_rows.append(pltpu.make_async_copy(heads(q_ref, yy * 2 + c), qg.at[0, yy, 0], loc.at[1 + yy]))
        own_rows.append(pltpu.make_async_copy(heads(g_ref, yy * 2 + c), qg.at[0, yy, 1], loc.at[1 + yy]))

    barrier = pltpu.get_barrier_semaphore()

    def greet(to_ctx, to_head):
        pl.semaphore_signal(barrier, inc=1, device_id=(to_ctx, to_head), device_id_type=MESH)

    @pl.loop(1, nh)
    def _(i):
        greet(ctx, lax.rem(j + i, nh))

    @pl.loop(1, nx)
    def _(i):
        @pl.loop(0, ny)
        def _(yy):
            greet(z * nx + lax.rem(x + i, nx), yy * 2 + c)

    @pl.loop(z + 1, nz)
    def _(to):
        greet(to * nx + x, j)

    @pl.when(ctx < nc - 1)
    def _():
        greet(ctx + 1, 0)

    for cp in own_rows:
        cp.start()

    follows = (j == 0) & (ctx > 0)
    pl.semaphore_wait(barrier, nh - 1 + (nx - 1) * ny + z + jnp.where(follows, nh, 0))

    @pl.loop(0, z)
    def _(to):
        pl.semaphore_signal(here.at[z], inc=1, device_id=(to * nx + x, j), device_id_type=MESH)

    own_tok = [
        pltpu.make_async_copy(heads(k_ref, j), tok.at[0, :, j], loc.at[1 + ny]),
        pltpu.make_async_copy(heads(v_ref, j), tok.at[1, :, j], loc.at[1 + ny]),
    ]
    for cp in own_tok:
        cp.start()

    @pl.loop(1, nh)
    def _(i):
        to = lax.rem(j + i, nh)
        remote(heads(k_ref, to), tok.at[0, :, j], tok_s, tok_r.at[j], ctx, to).start()
        remote(heads(v_ref, to), tok.at[1, :, j], tok_s, tok_r.at[j], ctx, to).start()

    @pl.when(follows)
    def _():
        @pl.loop(0, nh)
        def _(to):
            for which, src in ((0, k_ref), (1, v_ref)):
                remote(
                    src.at[pl.ds(to * hpd, hpd), pl.ds(0, EDGE)], ext.at[which, :, pl.ds(0, EDGE)],
                    ext_s, ext_r, ctx - 1, to,
                ).start()

    get_ids.wait()
    idb[y] = idv[:, pl.ds(pl.multiple_of(ctx * TB, LANES), TB)] - ctx * S

    @pl.loop(1, ny)
    def _(i):
        remote(idb.at[y], idb.at[y], id_s, id_r.at[y], ctx, lax.rem(y + i, ny) * 2 + c).start()

    @pl.loop(0, ny)
    def _(i):
        yy = lax.rem(y + i, ny)
        remote(heads(q_ref, yy * 2 + 1 - c), qg.at[1, yy, 0], sw_s, sw_r.at[yy], ctx, peer).start()
        remote(heads(g_ref, yy * 2 + 1 - c), qg.at[1, yy, 1], sw_s, sw_r.at[yy], ctx, peer).start()

    next_at = pl.multiple_of(jnp.minimum(ctx + 1, nc - 1) * TB, LANES)

    for h in range(hpd):
        main_ids = idv[h:h + 1, pl.ds(pl.multiple_of(ctx * TB, LANES), TB)] - ctx * S
        edge_ids = jnp.where(ctx < nc - 1, idv[h:h + 1, pl.ds(next_at, LANES)] - ctx * S, -1)
        main = (lax.broadcasted_iota(jnp.int32, (S, TB), 0) == main_ids).astype(f32)
        edge = (lax.broadcasted_iota(jnp.int32, (S, LANES), 0) == edge_ids).astype(f32)
        count = jnp.sum(main, axis=1, keepdims=True) + jnp.sum(edge, axis=1, keepdims=True)
        mains[h], edges[h] = main.astype(bf), edge.astype(bf)
        counts[h] = jnp.broadcast_to(count, (S, D))

    @pl.loop(1, nh)
    def _(i):
        arrived(tok.at[:, :, lax.rem(j + i, nh)], tok_r.at[lax.rem(j + i, nh)])

    own = tok.at[:, :, j]
    pltpu.make_async_copy(own, own, loc.at[1 + ny]).wait()

    @pl.when(ctx < nc - 1)
    def _():
        arrived(ext.at[:, :, pl.ds(0, EDGE)], ext_r)

    for h in range(hpd):
        for which in range(2):
            total = dot_nn(mains[h], tok[which, h].reshape(TB, D)) + dot_nn(edges[h], ext[which, h])
            kv[y, h, x, z, which] = (total / counts[h]).astype(bf)

    def spread(h, zs, where):
        blk = kv.at[y, h, x, zs]

        def give(to_x, to_y):
            to = to_x * ny + to_y
            remote(blk, blk, kp_s.at[to], kp_r.at[spot, h], z * nx + to_x, to_y * 2 + c).start()

        where(give)

    for h in range(hpd):
        @pl.loop(z + 1, nz)
        def _(i):
            to = nz + z - i

            if h == 0:
                pl.semaphore_wait(here.at[to], 1)

            blk = kv.at[y, h, x, z]
            remote(blk, blk, kz_s, kz_r.at[z, h], to * nx + x, j).start()

        spread(h, z, in_plane)


    @pl.loop(z + 1, nz)
    def _(zs):
        for yy in range(ny):
            for h in range(hpd):
                for xs in range(nx):
                    kv[yy, h, xs, zs] = jnp.zeros((2, S, D), bf)

    @pl.loop(1, ny)
    def _(i):
        yy = lax.rem(y + i, ny)
        arrived(idb.at[yy], id_r.at[yy])

    for t in range(2):
        core = c if t == 0 else 1 - c
        token = lax.broadcasted_iota(jnp.int32, (TB, R), 0) - (y * 2 + core) * T
        first = lax.broadcasted_iota(jnp.int32, (TB, R), 1) - token * group
        pick = ((first >= 0) & (first < group)).astype(f32).astype(bf)
        for yy in range(ny):
            for h in range(hpd):
                ids = idb[yy, h:h + 1].astype(f32).astype(bf)
                row = dot_nn(jnp.broadcast_to(ids, (16, TB)), pick)
                thr[yy, h, t] = row[:1].astype(jnp.int32)

    for h in range(hpd):
        def lift(frm_x, frm_y):
            frm = frm_x * ny + frm_y
            blk = kv.at[frm_y, h, frm_x, z]
            arrived(blk, kp_r.at[frm, h])

            @pl.loop(z + 1, nz)
            def _(i):
                to = nz + z - i
                remote(blk, blk, kd_s.at[frm], kd_r.at[frm, h], to * nx + x, j).start()

        apart(lift)

        @pl.loop(0, z)
        def _(i):
            zs = z - 1 - i
            arrived(kv.at[y, h, x, zs], kz_r.at[zs, h])
            spread(h, zs, near)

    def sum_near(h):
        def total(zb):
            out = part[y, h, x, zb].astype(f32)
            for i in range(1, nx):
                out += red[lax.rem(x + i, nx) * ny + y, h, zb].astype(f32)
            for i in range(1, ny):
                out += red[x * ny + lax.rem(y + i, ny), h, zb].astype(f32)
            return out

        def pass_on(zb):
            zout[h, zb] = total(zb).astype(bf)
            remote(zout.at[h, zb], zin.at[z, h], zs_s, zs_r.at[z, h], zb * nx + x, j).start()

        near(lambda fx, fy: arrived(red.at[fx * ny + fy, h, pl.ds(0, 1)], pt_r.at[fx * ny + fy, h, 0]))

        @pl.when(z > 0)
        def _():
            pass_on(0)
            near(lambda fx, fy: by_layers(lambda n: n > 1 and arrived(
                red.at[fx * ny + fy, h, pl.ds(1, n - 1)], pt_r.at[fx * ny + fy, h, 1]
            )))

        @pl.loop(1, z)
        def _(zb):
            pass_on(zb)

        acc[h] = total(z)

    def sum_apart(h):
        def cross(to_x, to_y):
            to = to_x * ny + to_y
            acc_far = part.at[to_y, h, to_x, z]

            by_layers(lambda n: n < nz and arrived(far.at[to, h, pl.ds(n, nz - n)], fz_r.at[to, h]))
            out = acc_far[...].astype(f32)
            for zb in range(1, nz):
                out += jnp.where(zb > z, far[to, h, zb].astype(f32), 0.0)
            fout[to, h] = out.astype(bf)
            remote(
                fout.at[to, h], fin.at[spot, h], fp_s.at[to], fp_r.at[spot, h], z * nx + to_x, to_y * 2 + c
            ).start()

        apart(cross)

    @pl.loop(0, hpd * ny)
    def _(u):
        h, k = u // ny, lax.rem(u, ny)
        yy = lax.rem(y + k, ny)

        @pl.when(h == 0)
        def _():
            pltpu.make_async_copy(qg.at[0, yy], qg.at[0, yy], loc.at[1 + yy]).wait()
            arrived(qg.at[1, yy], sw_r.at[yy])

        @pl.loop(0, nx)
        def _(i):
            xs = lax.rem(x + i, nx)

            @pl.when((i > 0) | (k > 0))
            def _():
                @pl.when((i == 0) | (k == 0))
                def _():
                    by_layers(lambda n: arrived(kv.at[yy, h, xs, pl.ds(0, n)], kp_r.at[xs * ny + yy, h]))

                @pl.when((i > 0) & (k > 0))
                def _():
                    by_layers(lambda n: n > 1 and arrived(
                        kv.at[yy, h, xs, pl.ds(0, n - 1)], kd_r.at[xs * ny + yy, h]
                    ))

        keys = kv[yy, h, :, :, 0].reshape(NS, D)
        vals = kv[yy, h, :, :, 1].reshape(NS, D)
        key_sum = val_sum = None
        for t in range(2):
            rows, grads = qg[t, yy, 0, h], qg[t, yy, 1, h]
            bar = thr[yy, h, t]
            raw_scores = dot_nt(keys, rows).reshape(nx, nz, S, R)
            slot = lax.broadcasted_iota(jnp.int32, (S, R), 0)
            scores = jnp.concatenate([
                jnp.where(slot <= bar - (zb * nx + xb - ctx) * S, raw_scores[xb, zb], neg_big)
                for xb in range(nx) for zb in range(nz)
            ], axis=0)
            top = jnp.max(scores, axis=0, keepdims=True)
            raw = jnp.exp2((scores - top) * (scale * math.log2(math.e)))
            weights = raw * (1.0 / jnp.sum(raw, axis=0, keepdims=True))
            low = weights.astype(bf)
            seen = dot_tn(vals, low).astype(bf).astype(f32)
            grads_t = grads.astype(f32).T
            row_dot = jnp.sum(grads_t * seen, axis=0, keepdims=True)
            seen_rows = seen.T.astype(bf)
            if t == 0:
                out_ref[(yy * 2 + c) * hpd + h] = seen_rows
            else:
                att[yy, h] = seen_rows
            slope = (weights * (dot_nt(vals, grads) - row_dot)).astype(bf)
            val_grad = dot_nn(low, grads)
            key_grad = dot_nn(slope, rows)
            key_sum = key_grad if key_sum is None else key_sum + key_grad
            val_sum = val_grad if val_sum is None else val_sum + val_grad
        part[yy, h, :, :, :, :D] = (key_sum * scale).astype(bf).reshape(nx, nz, S, D)
        part[yy, h, :, :, :, D:] = val_sum.astype(bf).reshape(nx, nz, S, D)

        @pl.loop(0, nx)
        def _(i):
            xs = lax.rem(x + i, nx)

            @pl.when((i > 0) != (k > 0))
            def _():
                def give(which, layers):
                    remote(
                        part.at[yy, h, xs, layers], red.at[spot, h, layers],
                        pt_s.at[xs * ny + yy], pt_r.at[spot, h, which], z * nx + xs, yy * 2 + c,
                    ).start()

                give(0, pl.ds(0, 1))
                by_layers(lambda n: n > 1 and give(1, pl.ds(1, n - 1)))

            @pl.when((i > 0) & (k > 0))
            def _():
                to = xs * ny + yy

                @pl.loop(0, z)
                def _(zb):
                    remote(
                        part.at[yy, h, xs, zb], far.at[to, h, z], fz_s.at[to], fz_r.at[to, h], zb * nx + x, j
                    ).start()

        remote(att.at[yy, h], out_ref.at[(yy * 2 + c) * hpd + h], at_s, at_r, ctx, peer).start()

        @pl.when((k == 0) & (h > 0))
        def _():
            sum_near(h - 1)

    sum_near(hpd - 1)
    for h in range(hpd):
        sum_apart(h)

    for h in range(hpd):
        @pl.loop(z + 1, nz)
        def _(frm):
            arrived(zin.at[frm, h], zs_r.at[frm, h])
            acc[h] += zin[frm, h].astype(f32)

        def take(frm_x, frm_y):
            frm = frm_x * ny + frm_y
            arrived(fin.at[frm, h], fp_r.at[frm, h])
            acc[h] += fin[frm, h].astype(f32)

        apart(take)
        mean = acc[h].astype(bf).astype(f32)
        twice = jnp.concatenate([counts[h], counts[h]], axis=1)
        unit = (mean / twice).astype(bf)
        spread_rows = dot_tn(mains[h], unit).astype(bf)
        for to in range(nh):
            tg[to, h] = spread_rows[to * T:(to + 1) * T]

        @pl.loop(1, nh)
        def _(i):
            to = lax.rem(j + i, nh)
            remote(tg.at[to, h], rt.at[j * hpd + h], tg_s, tg_r.at[j], ctx, to).start()

        tgx[h] = dot_tn(edges[h], unit)[:EDGE].astype(bf)

    @pl.when(ctx < nc - 1)
    def _():
        remote(tgx, heads(rx, j), tx_s, tx_r, ctx + 1, 0).start()

    rt[pl.ds(j * hpd, hpd)] = tg[j]

    sent(tok.at[:, :, pl.ds(0, nh - 1)], tok_s)

    @pl.when(follows)
    def _():
        sent(tok.at[:, :, :, pl.ds(0, EDGE)], ext_s)

    sent(idb.at[pl.ds(0, ny - 1)], id_s)
    sent(qg.at[1], sw_s)
    sent(att, at_s)
    arrived(att, at_r)
    for n in range(1, nz):
        @pl.when(z == nz - 1 - n)
        def _():
            sent(kv.at[y, :, x, pl.ds(0, n)], kz_s)
            apart(lambda fx, fy: sent(kv.at[fy, :, fx, pl.ds(0, n)], kd_s.at[fx * ny + fy]))

        @pl.when(z == n)
        def _():
            sent(zout.at[:, pl.ds(0, n)], zs_s)
            apart(lambda tx, ty: sent(part.at[ty, :, tx, pl.ds(0, n)], fz_s.at[tx * ny + ty]))

    def near_sent(to_x, to_y):
        to = to_x * ny + to_y

        def fn(n):
            sent(kv.at[y, :, x, pl.ds(0, n)], kp_s.at[to])
            sent(part.at[to_y, :, to_x, pl.ds(0, n)], pt_s.at[to])

        by_layers(fn)

    def apart_sent(to_x, to_y):
        to = to_x * ny + to_y
        sent(kv.at[y, :, x, 0], kp_s.at[to])
        sent(fout.at[to], fp_s.at[to])

    near(near_sent)
    apart(apart_sent)

    @pl.loop(1, nh)
    def _(i):
        frm = lax.rem(j + i, nh)
        arrived(heads(rt, frm), tg_r.at[frm])

    @pl.when(follows)
    def _():
        arrived(rx, tx_r)

    sent(tg.at[pl.ds(0, nh - 1)], tg_s)

    @pl.when(ctx < nc - 1)
    def _():
        sent(tgx, tx_s)


def hand_over(a_ref, t_ref, x_ref, a_out, k_out, v_out, kbuf, vbuf, sem):
    D = k_out.shape[-1]
    whole = pltpu.make_async_copy(a_ref, a_out, sem.at[0])
    whole.start()
    copies = [whole]
    for i, (buf, out) in enumerate(((kbuf, k_out), (vbuf, v_out))):
        cols = slice(i * D, (i + 1) * D)
        buf[...] = t_ref[:, :, cols].astype(f32)
        buf[:, :EDGE] += x_ref[:, :, cols].astype(f32)
        copies.append(pltpu.make_async_copy(buf, out, sem.at[1 + i]))
        copies[-1].start()
    for cp in copies:
        cp.wait()


def per_device(nc, nh, token_keys, token_values, queries, out_grad, slot_ids):
    heads_all, T, D = token_keys.shape
    group = queries.shape[2]
    hpd, context = slot_ids.shape
    R = queries.shape[1] * group
    TB = T * nh
    S = TB // RATIO
    ny = nh // 2
    nx = 2 ** ((nc.bit_length() - 1) // 2)
    nz = nc // nx
    plane = nx * ny
    dma = pltpu.SemaphoreType.DMA
    anywhere = pl.BlockSpec(memory_space=pl.ANY)
    vmem = pl.BlockSpec(memory_space=pltpu.VMEM)
    results = pl.pallas_call(
        functools.partial(kernel, (nc, nx, nh, hpd, T, R, S, D)),
        out_shape=(
            pltpu.VMEM((heads_all, R, D), bf),
            pltpu.VMEM((heads_all, T, 2 * D), bf),
            pltpu.VMEM((heads_all, EDGE, 2 * D), bf),
        ),
        in_specs=[anywhere] * 5,
        out_specs=(vmem, vmem, vmem),
        scratch_shapes=[
            pltpu.VMEM((hpd, context), jnp.int32),
            pltpu.VMEM((ny, hpd, TB), jnp.int32),
            pltpu.VMEM((ny, hpd, 2, 1, R), jnp.int32),
            pltpu.VMEM((hpd, S, TB), bf),
            pltpu.VMEM((hpd, S, LANES), bf),
            pltpu.VMEM((hpd, S, D), f32),
            pltpu.VMEM((2, ny, 2, hpd, R, D), bf),
            pltpu.VMEM((2, hpd, nh, T, D), bf),
            pltpu.VMEM((2, hpd, LANES, D), bf),
            pltpu.VMEM((ny, hpd, nx, nz, 2, S, D), bf),
            pltpu.VMEM((ny, hpd, R, D), bf),
            pltpu.VMEM((ny, hpd, nx, nz, S, 2 * D), bf),
            pltpu.VMEM((plane, hpd, nz, S, 2 * D), bf),
            pltpu.VMEM((hpd, nz, S, 2 * D), bf),
            pltpu.VMEM((nz, hpd, S, 2 * D), bf),
            pltpu.VMEM((plane, hpd, nz, S, 2 * D), bf),
            pltpu.VMEM((plane, hpd, S, 2 * D), bf),
            pltpu.VMEM((plane, hpd, S, 2 * D), bf),
            pltpu.VMEM((hpd, S, 2 * D), f32),
            pltpu.VMEM((nh, hpd, T, 2 * D), bf),
            pltpu.VMEM((hpd, EDGE, 2 * D), bf),
            pltpu.SemaphoreType.REGULAR((nz,)), dma((2 + ny,)),
            dma(()), dma((nh,)), dma(()), dma(()), dma(()), dma((ny,)), dma(()), dma((ny,)),
            dma(()), dma((nz, hpd)), dma((plane,)), dma((plane, hpd)), dma((plane,)), dma((plane, hpd)),
            dma((plane,)), dma((plane, hpd, 2)), dma(()), dma((nz, hpd)),
            dma((plane,)), dma((plane, hpd)), dma((plane,)), dma((plane, hpd)), dma(()), dma(()), dma(()), dma((nh,)), dma(()), dma(()),
        ],
        compiler_params=pltpu.CompilerParams(
            collective_id=0, has_side_effects=True, vmem_limit_bytes=60 << 20
        ),
    )(
        queries.reshape(heads_all, R, D), out_grad.reshape(heads_all, R, D),
        token_keys, token_values, slot_ids,
    )
    attended, grads, edges = [pltpu.with_memory_space_constraint(r, pltpu.VMEM) for r in results]
    attended, key_grad, value_grad = pl.pallas_call(
        hand_over,
        out_shape=(
            jax.ShapeDtypeStruct((heads_all, R, D), bf),
            jax.ShapeDtypeStruct((heads_all, T, D), f32),
            jax.ShapeDtypeStruct((heads_all, T, D), f32),
        ),
        in_specs=[vmem] * 3,
        out_specs=(anywhere,) * 3,
        scratch_shapes=[
            pltpu.VMEM((heads_all, T, D), f32), pltpu.VMEM((heads_all, T, D), f32), dma((3,)),
        ],
    )(attended, grads, edges)
    return attended.reshape(queries.shape), key_grad, value_grad


def solution(mesh):
    nc, nh = mesh.shape["ctx"], mesh.shape["head"]
    rows = P(None, ("ctx", "head"), None)
    grouped = P(None, ("ctx", "head"), None, None)
    return jax.shard_map(
        functools.partial(per_device, nc, nh),
        mesh=mesh,
        in_specs=(rows, rows, grouped, grouped, P("head", None)),
        out_specs=(grouped, rows, rows),
        check_vma=False,
    )
```

```python
import functools
import math

import jax
import jax.numpy as jnp
from jax import lax
from jax.experimental import pallas as pl
from jax.experimental.pallas import tpu as pltpu
from jax.sharding import PartitionSpec as P

RATIO = 4
EDGE = 16
LANES = 128
MESH = pl.DeviceIdType.MESH
neg_big = -1e30
bf, f32 = jnp.bfloat16, jnp.float32


def dot_nt(a, b):
    return lax.dot_general(a, b, (((1,), (1,)), ((), ())), preferred_element_type=f32)


def dot_tn(a, b):
    return lax.dot_general(a, b, (((0,), (0,)), ((), ())), preferred_element_type=f32)


def dot_nn(a, b):
    return lax.dot_general(a, b, (((1,), (0,)), ((), ())), preferred_element_type=f32)


def kernel(
    dims,
    q_ref, g_ref, k_ref, v_ref, id_ref,
    out_ref, rt, rx,
    idv, idb, thr, mains, edges, counts, qg, tok, ext, kv, att, part, red, zout, zin, far, fout, fin, straight, acc, tg, tgx,
    here, beside, loc, tok_s, tok_r, ext_s, ext_r, id_s, id_r, sw_s, sw_r,
    kz_s, kz_r, kp_s, kp_r, kd_s, kd_r, kr_s, st_s, st_r, pt_s, pt_r, zs_s, zs_r, fz_s, fz_r, fp_s, fp_r, at_s, at_r, tg_s, tg_r, tx_s, tx_r,
):
    nc, nx, nh, hpd, T, R, S, D = dims
    ny, nz = nh // 2, nc // nx
    plane = nx * ny
    TB = T * nh
    NS = nc * S
    group = R // T
    scale = 1.0 / math.sqrt(D)
    ctx = lax.axis_index("ctx")
    j = lax.axis_index("head")
    y, c = j // 2, lax.rem(j, 2)
    peer = y * 2 + 1 - c
    z, x = ctx // nx, lax.rem(ctx, nx)
    spot = x * ny + y

    def remote(src, dst, ssem, rsem, to_ctx, to_head):
        return pltpu.make_async_remote_copy(
            src_ref=src, dst_ref=dst, send_sem=ssem, recv_sem=rsem,
            device_id=(to_ctx, to_head), device_id_type=MESH,
        )

    def arrived(ref, sem):
        remote(ref, ref, sem, sem, ctx, peer).wait_recv()

    def sent(ref, sem):
        remote(ref, ref, sem, sem, ctx, peer).wait_send()

    def by_layers(fn):
        for n in range(1, nz + 1):
            @pl.when(z == n - 1)
            def _():
                fn(n)

    def heads(ref, owner):
        return ref.at[pl.ds(owner * hpd, hpd)]

    last = hpd - 1

    def near_x(fn):
        @pl.loop(1, nx)
        def _(i):
            fn(lax.rem(x + i, nx), y)

    def near_y(fn):
        @pl.loop(1, ny)
        def _(i):
            fn(x, lax.rem(y + i, ny))

    def near(fn):
        near_x(fn)
        near_y(fn)

    def apart(fn):
        @pl.loop(1, nx)
        def _(i):
            @pl.loop(1, ny)
            def _(e):
                fn(lax.rem(x + i, nx), lax.rem(y + e, ny))

    def in_plane(fn):
        near(fn)
        apart(fn)

    ext[...] = jnp.zeros_like(ext)
    rx[...] = jnp.zeros_like(rx)

    get_ids = pltpu.make_async_copy(id_ref, idv, loc.at[0])
    get_ids.start()
    own_rows = []
    for yy in range(ny):
        own_rows.append(pltpu.make_async_copy(heads(q_ref, yy * 2 + c), qg.at[0, yy, 0], loc.at[1 + yy]))
        own_rows.append(pltpu.make_async_copy(heads(g_ref, yy * 2 + c), qg.at[0, yy, 1], loc.at[1 + yy]))

    barrier = pltpu.get_barrier_semaphore()

    def greet(to_ctx, to_head):
        pl.semaphore_signal(barrier, inc=1, device_id=(to_ctx, to_head), device_id_type=MESH)

    @pl.loop(1, nh)
    def _(i):
        greet(ctx, lax.rem(j + i, nh))

    @pl.loop(x + 1, nx)
    def _(to_x):
        @pl.loop(0, ny)
        def _(yy):
            greet(z * nx + to_x, yy * 2 + c)

    @pl.loop(z + 1, nz)
    def _(to):
        greet(to * nx + x, j)

    @pl.when(ctx < nc - 1)
    def _():
        greet(ctx + 1, 0)

    for cp in own_rows:
        cp.start()

    follows = (j == 0) & (ctx > 0)
    pl.semaphore_wait(barrier, nh - 1 + x * ny + z + jnp.where(follows, nh, 0))

    @pl.loop(0, z)
    def _(to):
        pl.semaphore_signal(here.at[z], inc=1, device_id=(to * nx + x, j), device_id_type=MESH)

    @pl.loop(0, x)
    def _(to_x):
        @pl.loop(0, ny)
        def _(yy):
            pl.semaphore_signal(beside, inc=1, device_id=(z * nx + to_x, yy * 2 + c), device_id_type=MESH)

    own_tok = [
        pltpu.make_async_copy(heads(k_ref, j), tok.at[0, :, j], loc.at[1 + ny]),
        pltpu.make_async_copy(heads(v_ref, j), tok.at[1, :, j], loc.at[1 + ny]),
    ]
    for cp in own_tok:
        cp.start()

    @pl.loop(1, nh)
    def _(i):
        to = lax.rem(j + i, nh)
        remote(heads(k_ref, to), tok.at[0, :, j], tok_s, tok_r.at[j], ctx, to).start()
        remote(heads(v_ref, to), tok.at[1, :, j], tok_s, tok_r.at[j], ctx, to).start()

    @pl.when(follows)
    def _():
        @pl.loop(0, nh)
        def _(to):
            for which, src in ((0, k_ref), (1, v_ref)):
                remote(
                    src.at[pl.ds(to * hpd, hpd), pl.ds(0, EDGE)], ext.at[which, :, pl.ds(0, EDGE)],
                    ext_s, ext_r, ctx - 1, to,
                ).start()

    get_ids.wait()
    idb[y] = idv[:, pl.ds(pl.multiple_of(ctx * TB, LANES), TB)] - ctx * S

    @pl.loop(1, ny)
    def _(i):
        remote(idb.at[y], idb.at[y], id_s, id_r.at[y], ctx, lax.rem(y + i, ny) * 2 + c).start()

    @pl.loop(0, ny)
    def _(i):
        yy = lax.rem(y + i, ny)
        remote(heads(q_ref, yy * 2 + 1 - c), qg.at[1, yy, 0], sw_s, sw_r.at[yy], ctx, peer).start()
        remote(heads(g_ref, yy * 2 + 1 - c), qg.at[1, yy, 1], sw_s, sw_r.at[yy], ctx, peer).start()

    next_at = pl.multiple_of(jnp.minimum(ctx + 1, nc - 1) * TB, LANES)

    for h in range(hpd):
        main_ids = idv[h:h + 1, pl.ds(pl.multiple_of(ctx * TB, LANES), TB)] - ctx * S
        edge_ids = jnp.where(ctx < nc - 1, idv[h:h + 1, pl.ds(next_at, LANES)] - ctx * S, -1)
        main = (lax.broadcasted_iota(jnp.int32, (S, TB), 0) == main_ids).astype(f32)
        edge = (lax.broadcasted_iota(jnp.int32, (S, LANES), 0) == edge_ids).astype(f32)
        count = jnp.sum(main, axis=1, keepdims=True) + jnp.sum(edge, axis=1, keepdims=True)
        mains[h], edges[h] = main.astype(bf), edge.astype(bf)
        counts[h] = jnp.broadcast_to(count, (S, D))

    @pl.loop(1, nh)
    def _(i):
        arrived(tok.at[:, :, lax.rem(j + i, nh)], tok_r.at[lax.rem(j + i, nh)])

    own = tok.at[:, :, j]
    pltpu.make_async_copy(own, own, loc.at[1 + ny]).wait()

    @pl.when(ctx < nc - 1)
    def _():
        arrived(ext.at[:, :, pl.ds(0, EDGE)], ext_r)

    for h in range(hpd):
        for which in range(2):
            total = dot_nn(mains[h], tok[which, h].reshape(TB, D)) + dot_nn(edges[h], ext[which, h])
            kv[y, h, x, z, which] = (total / counts[h]).astype(bf)

    def spread(h, zs):
        blk = kv.at[y, h, x, zs]

        def give(sems, to_x, to_y):
            to = to_x * ny + to_y
            remote(blk, blk, sems.at[to], kp_r.at[spot, h], z * nx + to_x, to_y * 2 + c).start()

        near(functools.partial(give, kp_s))
        if h > 0:
            apart(functools.partial(give, kp_s))
        elif zs is z:
            apart(functools.partial(give, kr_s))

    @pl.when(x < nx - 1)
    def _():
        pl.semaphore_wait(beside, (nx - 1 - x) * ny)

    for h in range(hpd):
        @pl.loop(z + 1, nz)
        def _(i):
            to = nz + z - i

            if h == 0:
                pl.semaphore_wait(here.at[to], 1)

            blk = kv.at[y, h, x, z]

            remote(blk, blk, kz_s, kz_r.at[z, h], to * nx + x, j).start()

        spread(h, z)


    @pl.loop(1, ny)
    def _(i):
        yy = lax.rem(y + i, ny)
        arrived(idb.at[yy], id_r.at[yy])

    for t in range(2):
        core = c if t == 0 else 1 - c
        token = lax.broadcasted_iota(jnp.int32, (TB, R), 0) - (y * 2 + core) * T
        first = lax.broadcasted_iota(jnp.int32, (TB, R), 1) - token * group
        pick = ((first >= 0) & (first < group)).astype(f32).astype(bf)
        for yy in range(ny):
            for h in range(hpd):
                ids = idb[yy, h:h + 1].astype(f32).astype(bf)
                row = dot_nn(jnp.broadcast_to(ids, (16, TB)), pick)
                thr[yy, h, t] = row[:1].astype(jnp.int32)

    def lift(frm_x, frm_y):
        frm = frm_x * ny + frm_y
        blk = kv.at[frm_y, 0, frm_x, z]
        arrived(blk, kp_r.at[frm, 0])

        @pl.loop(z + 1, nz)
        def _(i):
            to = nz + z - i
            remote(blk, blk, kd_s.at[frm], kd_r.at[frm], to * nx + x, j).start()

    apart(lift)

    for h in range(hpd):
        @pl.loop(0, z)
        def _(i):
            zs = z - 1 - i
            arrived(kv.at[y, h, x, zs], kz_r.at[zs, h])
            spread(h, zs)

    def sum_plane(h, where):
        def total(zb):
            out = part[y, h, x, zb].astype(f32)
            if where is in_plane:
                for i in range(1, plane):
                    out += red[lax.rem(spot + i, plane), h, zb].astype(f32)
            else:
                for i in range(1, ny):
                    out += red[x * ny + lax.rem(y + i, ny), h, zb].astype(f32)
            return out

        def pass_on(zb):
            zout[h, zb] = total(zb).astype(bf)
            remote(zout.at[h, zb], zin.at[z, h], zs_s, zs_r.at[z, h], zb * nx + x, j).start()

        where(lambda fx, fy: arrived(red.at[fx * ny + fy, h, pl.ds(0, 1)], pt_r.at[fx * ny + fy, h, 0]))

        @pl.when(z > 0)
        def _():
            pass_on(0)
            where(lambda fx, fy: by_layers(lambda n: n > 1 and arrived(
                red.at[fx * ny + fy, h, pl.ds(1, n - 1)], pt_r.at[fx * ny + fy, h, 1]
            )))

        @pl.loop(1, z)
        def _(zb):
            pass_on(zb)

        acc[h] = total(z)

    def cross(to_x, to_y):
        to = to_x * ny + to_y
        by_layers(lambda n: n < nz and arrived(far.at[to, pl.ds(n, nz - n)], fz_r.at[to]))
        out = part[to_y, last, to_x, z].astype(f32)
        for zb in range(1, nz):
            out += jnp.where(zb > z, far[to, zb].astype(f32), 0.0)
        fout[to] = out.astype(bf)
        remote(fout.at[to], fin.at[spot], fp_s.at[to], fp_r.at[spot], z * nx + to_x, to_y * 2 + c).start()

    def attend(yy, h, n):
        keys = kv[yy, h, :, :n, 0].reshape(nx * n * S, D)
        vals = kv[yy, h, :, :n, 1].reshape(nx * n * S, D)
        key_sum = val_sum = None
        for t in range(2):
            rows, grads = qg[t, yy, 0, h], qg[t, yy, 1, h]
            bar = thr[yy, h, t]
            raw_scores = dot_nt(keys, rows).reshape(nx, n, S, R)
            slot = lax.broadcasted_iota(jnp.int32, (S, R), 0)
            scores = jnp.concatenate([
                jnp.where(slot <= bar - (zb * nx + xb - ctx) * S, raw_scores[xb, zb], neg_big)
                for xb in range(nx) for zb in range(n)
            ], axis=0)
            top = jnp.max(scores, axis=0, keepdims=True)
            raw = jnp.exp2((scores - top) * (scale * math.log2(math.e)))
            weights = raw * (1.0 / jnp.sum(raw, axis=0, keepdims=True))
            low = weights.astype(bf)
            seen = dot_tn(vals, low).astype(bf).astype(f32)
            grads_t = grads.astype(f32).T
            row_dot = jnp.sum(grads_t * seen, axis=0, keepdims=True)
            seen_rows = seen.T.astype(bf)
            if t == 0:
                out_ref[(yy * 2 + c) * hpd + h] = seen_rows
            else:
                att[yy, h] = seen_rows
            slope = (weights * (dot_nt(vals, grads) - row_dot)).astype(bf)
            val_grad = dot_nn(low, grads)
            key_grad = dot_nn(slope, rows)
            key_sum = key_grad if key_sum is None else key_sum + key_grad
            val_sum = val_grad if val_sum is None else val_sum + val_grad
        part[yy, h, :, :n, :, :D] = (key_sum * scale).astype(bf).reshape(nx, n, S, D)
        part[yy, h, :, :n, :, D:] = val_sum.astype(bf).reshape(nx, n, S, D)

    @pl.loop(0, hpd * ny)
    def _(u):
        h = u // ny
        k = lax.rem(u + jnp.where(h == last, 1, 0), ny)
        yy = lax.rem(y + k, ny)

        @pl.when(h == 0)
        def _():
            pltpu.make_async_copy(qg.at[0, yy], qg.at[0, yy], loc.at[1 + yy]).wait()
            arrived(qg.at[1, yy], sw_r.at[yy])

        @pl.loop(0, nx)
        def _(i):
            xs = lax.rem(x + i, nx)

            @pl.when((i > 0) | (k > 0))
            def _():
                @pl.when((i == 0) | (k == 0) | (h > 0))
                def _():
                    by_layers(lambda n: arrived(kv.at[yy, h, xs, pl.ds(0, n)], kp_r.at[xs * ny + yy, h]))

                @pl.when((i > 0) & (k > 0) & (h == 0))
                def _():
                    by_layers(lambda n: n > 1 and arrived(
                        kv.at[yy, h, xs, pl.ds(0, n - 1)], kd_r.at[xs * ny + yy]
                    ))

        by_layers(lambda n: attend(yy, h, n))

        @pl.loop(0, nx)
        def _(i):
            xs = lax.rem(x + i, nx)

            @pl.when(((i > 0) | (k > 0)) & ((h < last) | (i == 0)))
            def _():
                def give(which, layers):
                    remote(
                        part.at[yy, h, xs, layers], red.at[spot, h, layers],
                        pt_s.at[xs * ny + yy], pt_r.at[spot, h, which], z * nx + xs, yy * 2 + c,
                    ).start()

                give(0, pl.ds(0, 1))
                by_layers(lambda n: n > 1 and give(1, pl.ds(1, n - 1)))

            @pl.when((i > 0) & (k == 0) & (h == last))
            def _():
                @pl.loop(0, z + 1)
                def _(zb):
                    remote(
                        part.at[y, last, xs, zb], straight.at[x, z], st_s.at[xs], st_r.at[x], zb * nx + xs, j
                    ).start()

            @pl.when((i > 0) & (k > 0) & (h == last))
            def _():
                to = xs * ny + yy

                @pl.loop(0, z)
                def _(zb):
                    remote(
                        part.at[yy, last, xs, zb], far.at[to, z], fz_s.at[to], fz_r.at[to], zb * nx + x, j
                    ).start()

        remote(att.at[yy, h], out_ref.at[(yy * 2 + c) * hpd + h], at_s, at_r, ctx, peer).start()

        @pl.when((lax.rem(u, ny) == 0) & (h > 0))
        def _():
            sum_plane(h - 1, in_plane)

    sum_plane(last, near_y)
    apart(cross)

    for h in range(hpd):
        @pl.loop(z + 1, nz)
        def _(frm):
            arrived(zin.at[frm, h], zs_r.at[frm, h])
            acc[h] += zin[frm, h].astype(f32)

        if h == last:
            def take(frm_x, frm_y):
                frm = frm_x * ny + frm_y
                arrived(fin.at[frm], fp_r.at[frm])
                acc[h] += fin[frm].astype(f32)

            def add(frm_x, frm_y):
                by_layers(lambda n: arrived(straight.at[frm_x, pl.ds(n - 1, nz + 1 - n)], st_r.at[frm_x]))
                acc[h] += sum(
                    jnp.where(zb >= z, straight[frm_x, zb].astype(f32), 0.0) for zb in range(nz)
                )

            near_x(add)
            apart(take)

        mean = acc[h].astype(bf).astype(f32)
        twice = jnp.concatenate([counts[h], counts[h]], axis=1)
        unit = (mean / twice).astype(bf)
        spread_rows = dot_tn(mains[h], unit).astype(bf)
        for to in range(nh):
            tg[to, h] = spread_rows[to * T:(to + 1) * T]

        @pl.loop(1, nh)
        def _(i):
            to = lax.rem(j + i, nh)
            remote(tg.at[to, h], rt.at[j * hpd + h], tg_s, tg_r.at[j], ctx, to).start()

        tgx[h] = dot_tn(edges[h], unit)[:EDGE].astype(bf)

    @pl.when(ctx < nc - 1)
    def _():
        remote(tgx, heads(rx, j), tx_s, tx_r, ctx + 1, 0).start()

    rt[pl.ds(j * hpd, hpd)] = tg[j]

    sent(tok.at[:, :, pl.ds(0, nh - 1)], tok_s)

    @pl.when(follows)
    def _():
        sent(tok.at[:, :, :, pl.ds(0, EDGE)], ext_s)

    sent(idb.at[pl.ds(0, ny - 1)], id_s)
    sent(qg.at[1], sw_s)
    sent(att, at_s)
    arrived(att, at_r)
    for n in range(1, nz):
        @pl.when(z == nz - 1 - n)
        def _():
            sent(kv.at[y, :, x, pl.ds(0, n)], kz_s)
            apart(lambda fx, fy: sent(kv.at[fy, 0, fx, pl.ds(0, n)], kd_s.at[fx * ny + fy]))

        @pl.when(z == n)
        def _():
            sent(zout.at[:, pl.ds(0, n)], zs_s)
            apart(lambda tx, ty: sent(part.at[ty, last, tx, pl.ds(0, n)], fz_s.at[tx * ny + ty]))

    def near_sent(to_x, to_y):
        to = to_x * ny + to_y
        by_layers(lambda n: sent(kv.at[y, :, x, pl.ds(0, n)], kp_s.at[to]))

    def parts_sent(to_x, to_y, count):
        by_layers(lambda n: sent(part.at[to_y, pl.ds(0, count), to_x, pl.ds(0, n)], pt_s.at[to_x * ny + to_y]))

    near_y(lambda tx, ty: parts_sent(tx, ty, hpd))
    if hpd > 1:
        near_x(lambda tx, ty: parts_sent(tx, ty, hpd - 1))
        apart(lambda tx, ty: parts_sent(tx, ty, hpd - 1))
    near_x(lambda tx, ty: by_layers(lambda n: sent(part.at[y, last, tx, pl.ds(0, n)], st_s.at[tx])))

    def apart_sent(to_x, to_y):
        to = to_x * ny + to_y
        sent(kv.at[y, 0, x, 0], kr_s.at[to])
        if hpd > 1:
            by_layers(lambda n: sent(kv.at[y, pl.ds(1, hpd - 1), x, pl.ds(0, n)], kp_s.at[to]))
        sent(fout.at[to], fp_s.at[to])

    near(near_sent)
    apart(apart_sent)

    @pl.loop(1, nh)
    def _(i):
        frm = lax.rem(j + i, nh)
        arrived(heads(rt, frm), tg_r.at[frm])

    @pl.when(follows)
    def _():
        arrived(rx, tx_r)

    sent(tg.at[pl.ds(0, nh - 1)], tg_s)

    @pl.when(ctx < nc - 1)
    def _():
        sent(tgx, tx_s)


def hand_over(a_ref, t_ref, x_ref, a_out, k_out, v_out, kbuf, vbuf, sem):
    D = k_out.shape[-1]
    whole = pltpu.make_async_copy(a_ref, a_out, sem.at[0])
    whole.start()
    copies = [whole]
    for i, (buf, out) in enumerate(((kbuf, k_out), (vbuf, v_out))):
        cols = slice(i * D, (i + 1) * D)
        buf[...] = t_ref[:, :, cols].astype(f32)
        buf[:, :EDGE] += x_ref[:, :, cols].astype(f32)
        copies.append(pltpu.make_async_copy(buf, out, sem.at[1 + i]))
        copies[-1].start()
    for cp in copies:
        cp.wait()


def per_device(nc, nh, token_keys, token_values, queries, out_grad, slot_ids):
    heads_all, T, D = token_keys.shape
    group = queries.shape[2]
    hpd, context = slot_ids.shape
    R = queries.shape[1] * group
    TB = T * nh
    S = TB // RATIO
    ny = nh // 2
    nx = 2 ** ((nc.bit_length() - 1) // 2)
    nz = nc // nx
    plane = nx * ny
    dma = pltpu.SemaphoreType.DMA
    anywhere = pl.BlockSpec(memory_space=pl.ANY)
    vmem = pl.BlockSpec(memory_space=pltpu.VMEM)
    results = pl.pallas_call(
        functools.partial(kernel, (nc, nx, nh, hpd, T, R, S, D)),
        out_shape=(
            pltpu.VMEM((heads_all, R, D), bf),
            pltpu.VMEM((heads_all, T, 2 * D), bf),
            pltpu.VMEM((heads_all, EDGE, 2 * D), bf),
        ),
        in_specs=[anywhere] * 5,
        out_specs=(vmem, vmem, vmem),
        scratch_shapes=[
            pltpu.VMEM((hpd, context), jnp.int32),
            pltpu.VMEM((ny, hpd, TB), jnp.int32),
            pltpu.VMEM((ny, hpd, 2, 1, R), jnp.int32),
            pltpu.VMEM((hpd, S, TB), bf),
            pltpu.VMEM((hpd, S, LANES), bf),
            pltpu.VMEM((hpd, S, D), f32),
            pltpu.VMEM((2, ny, 2, hpd, R, D), bf),
            pltpu.VMEM((2, hpd, nh, T, D), bf),
            pltpu.VMEM((2, hpd, LANES, D), bf),
            pltpu.VMEM((ny, hpd, nx, nz, 2, S, D), bf),
            pltpu.VMEM((ny, hpd, R, D), bf),
            pltpu.VMEM((ny, hpd, nx, nz, S, 2 * D), bf),
            pltpu.VMEM((plane, hpd, nz, S, 2 * D), bf),
            pltpu.VMEM((hpd, nz, S, 2 * D), bf),
            pltpu.VMEM((nz, hpd, S, 2 * D), bf),
            pltpu.VMEM((plane, nz, S, 2 * D), bf),
            pltpu.VMEM((plane, S, 2 * D), bf),
            pltpu.VMEM((plane, S, 2 * D), bf),
            pltpu.VMEM((nx, nz, S, 2 * D), bf),
            pltpu.VMEM((hpd, S, 2 * D), f32),
            pltpu.VMEM((nh, hpd, T, 2 * D), bf),
            pltpu.VMEM((hpd, EDGE, 2 * D), bf),
            pltpu.SemaphoreType.REGULAR((nz,)), pltpu.SemaphoreType.REGULAR(()), dma((2 + ny,)),
            dma(()), dma((nh,)), dma(()), dma(()), dma(()), dma((ny,)), dma(()), dma((ny,)),
            dma(()), dma((nz, hpd)), dma((plane,)), dma((plane, hpd)), dma((plane,)), dma((plane,)),
            dma((plane,)), dma((nx,)), dma((nx,)), dma((plane,)), dma((plane, hpd, 2)), dma(()), dma((nz, hpd)),
            dma((plane,)), dma((plane,)), dma((plane,)), dma((plane,)),
            dma(()), dma(()), dma(()), dma((nh,)), dma(()), dma(()),
        ],
        compiler_params=pltpu.CompilerParams(
            collective_id=0, has_side_effects=True, vmem_limit_bytes=60 << 20
        ),
    )(
        queries.reshape(heads_all, R, D), out_grad.reshape(heads_all, R, D),
        token_keys, token_values, slot_ids,
    )
    attended, grads, edges = [pltpu.with_memory_space_constraint(r, pltpu.VMEM) for r in results]
    attended, key_grad, value_grad = pl.pallas_call(
        hand_over,
        out_shape=(
            jax.ShapeDtypeStruct((heads_all, R, D), bf),
            jax.ShapeDtypeStruct((heads_all, T, D), f32),
            jax.ShapeDtypeStruct((heads_all, T, D), f32),
        ),
        in_specs=[vmem] * 3,
        out_specs=(anywhere,) * 3,
        scratch_shapes=[
            pltpu.VMEM((heads_all, T, D), f32), pltpu.VMEM((heads_all, T, D), f32), dma((3,)),
        ],
    )(attended, grads, edges)
    return attended.reshape(queries.shape), key_grad, value_grad


def solution(mesh):
    nc, nh = mesh.shape["ctx"], mesh.shape["head"]
    rows = P(None, ("ctx", "head"), None)
    grouped = P(None, ("ctx", "head"), None, None)
    return jax.shard_map(
        functools.partial(per_device, nc, nh),
        mesh=mesh,
        in_specs=(rows, rows, grouped, grouped, P("head", None)),
        out_specs=(grouped, rows, rows),
        check_vma=False,
    )
```

```python
import functools
import math

import jax
import jax.numpy as jnp
from jax import lax
from jax.experimental import pallas as pl
from jax.experimental.pallas import tpu as pltpu
from jax.sharding import PartitionSpec as P

RATIO = 4
EDGE = 16
LANES = 128
MESH = pl.DeviceIdType.MESH
neg_big = -1e30
bf, f32 = jnp.bfloat16, jnp.float32


def dot_nt(a, b):
    return lax.dot_general(a, b, (((1,), (1,)), ((), ())), preferred_element_type=f32)


def dot_tn(a, b):
    return lax.dot_general(a, b, (((0,), (0,)), ((), ())), preferred_element_type=f32)


def dot_nn(a, b):
    return lax.dot_general(a, b, (((1,), (0,)), ((), ())), preferred_element_type=f32)


def kernel(
    dims,
    q_ref, g_ref, k_ref, v_ref, id_ref,
    out_ref, rt, rx,
    idv, idb, thr, mains, edges, counts, qg, tok, ext, kv, att, raws, lows, part, red, zout, zin, straight, acc, tg, tgx,
    here, beside, loc, tok_s, tok_r, ext_s, ext_r, id_s, id_r, sw_s, sw_r,
    kz_s, kz_r, kp_s, kp_r, kd_s, kd_r, st_s, st_r, pt_s, pt_r, zs_s, zs_r, at_s, at_r, tg_s, tg_r, tx_s, tx_r,
):
    nc, nx, nh, hpd, T, R, S, D = dims
    ny, nz = nh // 2, nc // nx
    plane = nx * ny
    TB = T * nh
    NS = nc * S
    group = R // T
    scale = 1.0 / math.sqrt(D)
    ctx = lax.axis_index("ctx")
    j = lax.axis_index("head")
    y, c = j // 2, lax.rem(j, 2)
    peer = y * 2 + 1 - c
    z, x = ctx // nx, lax.rem(ctx, nx)
    spot = x * ny + y

    def remote(src, dst, ssem, rsem, to_ctx, to_head):
        return pltpu.make_async_remote_copy(
            src_ref=src, dst_ref=dst, send_sem=ssem, recv_sem=rsem,
            device_id=(to_ctx, to_head), device_id_type=MESH,
        )

    def arrived(ref, sem):
        remote(ref, ref, sem, sem, ctx, peer).wait_recv()

    def sent(ref, sem):
        remote(ref, ref, sem, sem, ctx, peer).wait_send()

    def by_layers(fn):
        for n in range(1, nz + 1):
            @pl.when(z == n - 1)
            def _():
                fn(n)

    def heads(ref, owner):
        return ref.at[pl.ds(owner * hpd, hpd)]

    last = hpd - 1
    groups = min(3, nz)

    def near_x(fn):
        @pl.loop(1, nx)
        def _(i):
            fn(lax.rem(x + i, nx), y)

    def near_y(fn):
        @pl.loop(1, ny)
        def _(i):
            fn(x, lax.rem(y + i, ny))

    def near(fn):
        near_x(fn)
        near_y(fn)

    def apart(fn):
        @pl.loop(1, nx)
        def _(i):
            @pl.loop(1, ny)
            def _(e):
                fn(lax.rem(x + i, nx), lax.rem(y + e, ny))

    def in_plane(fn):
        near(fn)
        apart(fn)

    ext[...] = jnp.zeros_like(ext)
    rx[...] = jnp.zeros_like(rx)

    get_ids = pltpu.make_async_copy(id_ref, idv, loc.at[0])
    get_ids.start()
    own_rows = []
    for yy in range(ny):
        own_rows.append(pltpu.make_async_copy(heads(q_ref, yy * 2 + c), qg.at[0, yy, 0], loc.at[1 + yy]))
        own_rows.append(pltpu.make_async_copy(heads(g_ref, yy * 2 + c), qg.at[0, yy, 1], loc.at[1 + yy]))

    barrier = pltpu.get_barrier_semaphore()

    def greet(to_ctx, to_head):
        pl.semaphore_signal(barrier, inc=1, device_id=(to_ctx, to_head), device_id_type=MESH)

    @pl.loop(1, nh)
    def _(i):
        greet(ctx, lax.rem(j + i, nh))

    @pl.loop(x + 1, nx)
    def _(to_x):
        @pl.loop(0, ny)
        def _(yy):
            greet(z * nx + to_x, yy * 2 + c)

    @pl.loop(z + 1, nz)
    def _(to):
        greet(to * nx + x, j)

    @pl.when(ctx < nc - 1)
    def _():
        greet(ctx + 1, 0)

    for cp in own_rows:
        cp.start()

    follows = (j == 0) & (ctx > 0)
    pl.semaphore_wait(barrier, nh - 1 + x * ny + z + jnp.where(follows, nh, 0))

    @pl.loop(0, z)
    def _(to):
        pl.semaphore_signal(here.at[z], inc=1, device_id=(to * nx + x, j), device_id_type=MESH)

    @pl.loop(0, x)
    def _(to_x):
        @pl.loop(0, ny)
        def _(yy):
            pl.semaphore_signal(beside, inc=1, device_id=(z * nx + to_x, yy * 2 + c), device_id_type=MESH)

    own_tok = [
        pltpu.make_async_copy(heads(k_ref, j), tok.at[0, :, j], loc.at[1 + ny]),
        pltpu.make_async_copy(heads(v_ref, j), tok.at[1, :, j], loc.at[1 + ny]),
    ]
    for cp in own_tok:
        cp.start()

    @pl.loop(1, nh)
    def _(i):
        to = lax.rem(j + i, nh)
        remote(heads(k_ref, to), tok.at[0, :, j], tok_s, tok_r.at[j], ctx, to).start()
        remote(heads(v_ref, to), tok.at[1, :, j], tok_s, tok_r.at[j], ctx, to).start()

    @pl.when(follows)
    def _():
        @pl.loop(0, nh)
        def _(to):
            for which, src in ((0, k_ref), (1, v_ref)):
                remote(
                    src.at[pl.ds(to * hpd, hpd), pl.ds(0, EDGE)], ext.at[which, :, pl.ds(0, EDGE)],
                    ext_s, ext_r, ctx - 1, to,
                ).start()

    get_ids.wait()
    idb[y] = idv[:, pl.ds(pl.multiple_of(ctx * TB, LANES), TB)] - ctx * S

    @pl.loop(1, ny)
    def _(i):
        remote(idb.at[y], idb.at[y], id_s, id_r.at[y], ctx, lax.rem(y + i, ny) * 2 + c).start()

    @pl.loop(0, ny)
    def _(i):
        yy = lax.rem(y + i, ny)
        remote(heads(q_ref, yy * 2 + 1 - c), qg.at[1, yy, 0], sw_s, sw_r.at[yy], ctx, peer).start()
        remote(heads(g_ref, yy * 2 + 1 - c), qg.at[1, yy, 1], sw_s, sw_r.at[yy], ctx, peer).start()

    next_at = pl.multiple_of(jnp.minimum(ctx + 1, nc - 1) * TB, LANES)

    for h in range(hpd):
        main_ids = idv[h:h + 1, pl.ds(pl.multiple_of(ctx * TB, LANES), TB)] - ctx * S
        edge_ids = jnp.where(ctx < nc - 1, idv[h:h + 1, pl.ds(next_at, LANES)] - ctx * S, -1)
        main = (lax.broadcasted_iota(jnp.int32, (S, TB), 0) == main_ids).astype(f32)
        edge = (lax.broadcasted_iota(jnp.int32, (S, LANES), 0) == edge_ids).astype(f32)
        count = jnp.sum(main, axis=1, keepdims=True) + jnp.sum(edge, axis=1, keepdims=True)
        mains[h], edges[h] = main.astype(bf), edge.astype(bf)
        counts[h] = jnp.broadcast_to(count, (S, D))

    @pl.loop(1, nh)
    def _(i):
        arrived(tok.at[:, :, lax.rem(j + i, nh)], tok_r.at[lax.rem(j + i, nh)])

    own = tok.at[:, :, j]
    pltpu.make_async_copy(own, own, loc.at[1 + ny]).wait()

    @pl.when(ctx < nc - 1)
    def _():
        arrived(ext.at[:, :, pl.ds(0, EDGE)], ext_r)

    for h in range(hpd):
        for which in range(2):
            total = dot_nn(mains[h], tok[which, h].reshape(TB, D)) + dot_nn(edges[h], ext[which, h])
            kv[y, h, x, z, which] = (total / counts[h]).astype(bf)

    def spread(h, zs):
        blk = kv.at[y, h, x, zs]

        def give(sems, to_x, to_y):
            to = to_x * ny + to_y
            remote(blk, blk, sems.at[to], kp_r.at[spot, h], z * nx + to_x, to_y * 2 + c).start()

        near(functools.partial(give, kp_s))
        if zs is z:
            apart(functools.partial(give, kp_s))

    @pl.when(x < nx - 1)
    def _():
        pl.semaphore_wait(beside, (nx - 1 - x) * ny)

    @pl.loop(z + 1, nz)
    def _(i):
        to = nz + z - i
        pl.semaphore_wait(here.at[to], 1)
        for h in range(hpd):
            blk = kv.at[y, h, x, z]
            remote(blk, blk, kz_s, kz_r.at[z, h], to * nx + x, j).start()

    for h in range(hpd):
        spread(h, z)

    for h in range(hpd):
        def lift(frm_x, frm_y):
            frm = frm_x * ny + frm_y
            blk = kv.at[frm_y, h, frm_x, z]
            arrived(blk, kp_r.at[frm, h])

            @pl.loop(z + 1, nz)
            def _(i):
                to = nz + z - i
                remote(blk, blk, kd_s.at[frm], kd_r.at[frm, h], to * nx + x, j).start()

        apart(lift)

        @pl.loop(0, z)
        def _(i):
            zs = z - 1 - i
            arrived(kv.at[y, h, x, zs], kz_r.at[zs, h])
            spread(h, zs)

    @pl.loop(1, ny)
    def _(i):
        yy = lax.rem(y + i, ny)
        arrived(idb.at[yy], id_r.at[yy])

    for t in range(2):
        core = c if t == 0 else 1 - c
        token = lax.broadcasted_iota(jnp.int32, (TB, R), 0) - (y * 2 + core) * T
        first = lax.broadcasted_iota(jnp.int32, (TB, R), 1) - token * group
        pick = ((first >= 0) & (first < group)).astype(f32).astype(bf)
        for yy in range(ny):
            for h in range(hpd):
                ids = idb[yy, h:h + 1].astype(f32).astype(bf)
                row = dot_nn(jnp.broadcast_to(ids, (16, TB)), pick)
                thr[yy, h, t] = row[:1].astype(jnp.int32)

    def total(h, zb):
        out = part[y, h, x, zb].astype(f32)
        for i in range(nx):
            for e in range(ny):
                if i + e > 0 and (h < last or e > 0):
                    out += red[lax.rem(x + i, nx) * ny + lax.rem(y + e, ny), h, zb].astype(f32)
        return out

    def givers(h, fn):
        near_y(fn)
        apart(fn)
        if h < last:
            near_x(fn)

    def pass_on(h, zb):
        zout[h, zb] = total(h, zb).astype(bf)
        remote(zout.at[h, zb], zin.at[z, h], zs_s, zs_r.at[z, h], zb * nx + x, j).start()

    def group_of(g, n):
        first = min(g, n)
        return pl.ds(first, (n if g == groups - 1 else min(g + 1, n)) - first)

    def give(h, yy, xs, g):
        def send(layers):
            remote(
                part.at[yy, h, xs, layers], red.at[spot, h, layers],
                pt_s.at[xs * ny + yy], pt_r.at[spot, h, g], z * nx + xs, yy * 2 + c,
            ).start()

        by_layers(lambda n: n > g and send(group_of(g, n)))

    def give_all(h, yy, own, g):
        @pl.loop(own, nx)
        def _(i):
            give(h, yy, lax.rem(x + i, nx), g)

    def give_straight(g):
        def send(zb, to_x):
            remote(
                part.at[y, last, to_x, zb], straight.at[x, z], st_s.at[to_x], st_r.at[x], zb * nx + to_x, j
            ).start()

        near_x(lambda tx, ty: by_layers(lambda n: n > g and [
            send(zb, tx) for zb in range(n)[g:(n if g == groups - 1 else g + 1)]
        ]))

    def sum_plane():
        for g in range(groups):
            for h in range(hpd):
                givers(h, lambda fx, fy: by_layers(lambda n: n > g and arrived(
                    red.at[fx * ny + fy, h, group_of(g, n)], pt_r.at[fx * ny + fy, h, g]
                )))

                @pl.loop(g, jnp.minimum(z, nz if g == groups - 1 else g + 1))
                def _(zb):
                    pass_on(h, zb)

                @pl.when((z == g) | ((z > g) & (g == groups - 1)))
                def _():
                    acc[h] = total(h, z)

                if h == 0 and g == 0:
                    for rest in range(1, groups):
                        give_straight(rest)

    def attend(yy, h, n):
        width, step = nx * n * S, 2 * S
        keys = kv[yy, h, :, :n, 0].reshape(width, D)
        vals = kv[yy, h, :, :n, 1].reshape(width, D)
        chunks = [slice(at, at + step) for at in range(0, width, step)]
        slot = lax.broadcasted_iota(jnp.int32, (S, R), 0)

        def score(t):
            top = None
            for at in chunks:
                scores = dot_nt(keys[at], qg[t, yy, 0, h])
                for half in range(2):
                    xb, zb = divmod(at.start // S + half, n)
                    part_scores = scores[half * S:(half + 1) * S]
                    if zb == n - 1:
                        bar = thr[yy, h, t] - (zb * nx + xb - ctx) * S
                        part_scores = jnp.where(slot <= bar, part_scores, neg_big)
                    begin = at.start + half * S
                    raws[t, begin:begin + S] = part_scores
                    high = jnp.max(part_scores, axis=0, keepdims=True)
                    top = high if top is None else jnp.maximum(top, high)
            return top

        def power(t, top):
            whole = None
            for at in chunks:
                raw = jnp.exp2((raws[t, at] - top) * (scale * math.log2(math.e)))
                raws[t, at] = raw
                some = jnp.sum(raw, axis=0, keepdims=True)
                whole = some if whole is None else whole + some
            return 1.0 / whole

        def look(t, inverse):
            for at in chunks:
                lows[t, 0, at] = (raws[t, at] * inverse).astype(bf)
            seen = dot_tn(vals, lows[t, 0, :width]).astype(bf)
            if t == 0:
                out_ref[(yy * 2 + c) * hpd + h] = seen.T
            else:
                att[yy, h] = seen.T
            return jnp.sum(qg[t, yy, 1, h].T.astype(f32) * seen.astype(f32), axis=0, keepdims=True)

        def slopes(t, inverse, row_dot):
            rows, grads = qg[t, yy, 0, h], qg[t, yy, 1, h]
            for at in chunks:
                lows[t, 1, at] = ((raws[t, at] * inverse) * (dot_nt(vals[at], grads) - row_dot)).astype(bf)
            return dot_nn(lows[t, 1, :width], rows), dot_nn(lows[t, 0, :width], grads)

        tops = [score(t) for t in range(2)]
        inverses = [power(t, tops[t]) for t in range(2)]
        row_dots = [look(t, inverses[t]) for t in range(2)]
        grads = [slopes(t, inverses[t], row_dots[t]) for t in range(2)]
        part[yy, h, :, :n, :, :D] = ((grads[0][0] + grads[1][0]) * scale).astype(bf).reshape(nx, n, S, D)
        part[yy, h, :, :n, :, D:] = (grads[0][1] + grads[1][1]).astype(bf).reshape(nx, n, S, D)

    @pl.loop(0, hpd * ny)
    def _(u):
        h = u // ny
        k = lax.rem(u + jnp.where(h == last, 1, 0), ny)
        yy = lax.rem(y + k, ny)

        @pl.when(h == 0)
        def _():
            pltpu.make_async_copy(qg.at[0, yy], qg.at[0, yy], loc.at[1 + yy]).wait()
            arrived(qg.at[1, yy], sw_r.at[yy])

        @pl.loop(0, nx)
        def _(i):
            xs = lax.rem(x + i, nx)

            @pl.when((i > 0) | (k > 0))
            def _():
                @pl.when((i == 0) | (k == 0))
                def _():
                    by_layers(lambda n: arrived(kv.at[yy, h, xs, pl.ds(0, n)], kp_r.at[xs * ny + yy, h]))

                @pl.when((i > 0) & (k > 0))
                def _():
                    by_layers(lambda n: n > 1 and arrived(
                        kv.at[yy, h, xs, pl.ds(0, n - 1)], kd_r.at[xs * ny + yy, h]
                    ))

        by_layers(lambda n: attend(yy, h, n))

        @pl.when((k == 0) & (h == last))
        def _():
            give_straight(0)

        @pl.when((k > 0) | (h < last))
        def _():
            own = jnp.where(k == 0, 1, 0)
            give_all(h, yy, own, 0)

            @pl.when((h < last) & (k < ny - 1))
            def _():
                for g in range(1, groups):
                    give_all(h, yy, own, g)

            @pl.when((h == last) & (k == ny - 1))
            def _():
                for g in range(1, groups):
                    for hh in range(hpd):
                        @pl.loop(1, ny)
                        def _(e):
                            @pl.when((hh == last) | (e == ny - 1))
                            def _():
                                give_all(hh, lax.rem(y + e, ny), 0, g)

        remote(att.at[yy, h], out_ref.at[(yy * 2 + c) * hpd + h], at_s, at_r, ctx, peer).start()

    sum_plane()

    for h in range(hpd):
        @pl.loop(z + 1, nz)
        def _(frm):
            arrived(zin.at[frm, h], zs_r.at[frm, h])
            acc[h] += zin[frm, h].astype(f32)

        if h == last:
            def add(frm_x, frm_y):
                by_layers(lambda n: arrived(straight.at[frm_x, pl.ds(n - 1, nz + 1 - n)], st_r.at[frm_x]))
                acc[h] += sum(
                    jnp.where(zb >= z, straight[frm_x, zb].astype(f32), 0.0) for zb in range(nz)
                )

            near_x(add)

        mean = acc[h].astype(bf).astype(f32)
        twice = jnp.concatenate([counts[h], counts[h]], axis=1)
        unit = (mean / twice).astype(bf)
        spread_rows = dot_tn(mains[h], unit).astype(bf)
        for to in range(nh):
            tg[to, h] = spread_rows[to * T:(to + 1) * T]

        @pl.loop(1, nh)
        def _(i):
            to = lax.rem(j + i, nh)
            remote(tg.at[to, h], rt.at[j * hpd + h], tg_s, tg_r.at[j], ctx, to).start()

        tgx[h] = dot_tn(edges[h], unit)[:EDGE].astype(bf)

    @pl.when(ctx < nc - 1)
    def _():
        remote(tgx, heads(rx, j), tx_s, tx_r, ctx + 1, 0).start()

    rt[pl.ds(j * hpd, hpd)] = tg[j]

    sent(tok.at[:, :, pl.ds(0, nh - 1)], tok_s)

    @pl.when(follows)
    def _():
        sent(tok.at[:, :, :, pl.ds(0, EDGE)], ext_s)

    sent(idb.at[pl.ds(0, ny - 1)], id_s)
    sent(qg.at[1], sw_s)
    sent(att, at_s)
    arrived(att, at_r)
    for n in range(1, nz):
        @pl.when(z == nz - 1 - n)
        def _():
            sent(kv.at[y, :, x, pl.ds(0, n)], kz_s)
            apart(lambda fx, fy: sent(kv.at[fy, :, fx, pl.ds(0, n)], kd_s.at[fx * ny + fy]))

        @pl.when(z == n)
        def _():
            sent(zout.at[:, pl.ds(0, n)], zs_s)

    def near_sent(to_x, to_y):
        to = to_x * ny + to_y
        by_layers(lambda n: sent(kv.at[y, :, x, pl.ds(0, n)], kp_s.at[to]))

    def parts_sent(to_x, to_y, count):
        by_layers(lambda n: sent(part.at[to_y, pl.ds(0, count), to_x, pl.ds(0, n)], pt_s.at[to_x * ny + to_y]))

    near_y(lambda tx, ty: parts_sent(tx, ty, hpd))
    if hpd > 1:
        near_x(lambda tx, ty: parts_sent(tx, ty, hpd - 1))

    apart(lambda tx, ty: parts_sent(tx, ty, hpd))
    near_x(lambda tx, ty: by_layers(lambda n: sent(part.at[y, last, tx, pl.ds(0, n)], st_s.at[tx])))

    def apart_sent(to_x, to_y):
        sent(kv.at[y, :, x, 0], kp_s.at[to_x * ny + to_y])

    near(near_sent)
    apart(apart_sent)

    @pl.loop(1, nh)
    def _(i):
        frm = lax.rem(j + i, nh)
        arrived(heads(rt, frm), tg_r.at[frm])

    @pl.when(follows)
    def _():
        arrived(rx, tx_r)

    sent(tg.at[pl.ds(0, nh - 1)], tg_s)

    @pl.when(ctx < nc - 1)
    def _():
        sent(tgx, tx_s)


def hand_over(a_ref, t_ref, x_ref, a_out, k_out, v_out, kbuf, vbuf, sem):
    D = k_out.shape[-1]
    whole = pltpu.make_async_copy(a_ref, a_out, sem.at[0])
    whole.start()
    copies = [whole]
    for i, (buf, out) in enumerate(((kbuf, k_out), (vbuf, v_out))):
        cols = slice(i * D, (i + 1) * D)
        buf[...] = t_ref[:, :, cols].astype(f32)
        buf[:, :EDGE] += x_ref[:, :, cols].astype(f32)
        copies.append(pltpu.make_async_copy(buf, out, sem.at[1 + i]))
        copies[-1].start()
    for cp in copies:
        cp.wait()


def per_device(nc, nh, token_keys, token_values, queries, out_grad, slot_ids):
    heads_all, T, D = token_keys.shape
    group = queries.shape[2]
    hpd, context = slot_ids.shape
    R = queries.shape[1] * group
    TB = T * nh
    S = TB // RATIO
    ny = nh // 2
    nx = 2 ** ((nc.bit_length() - 1) // 2)
    nz = nc // nx
    plane = nx * ny
    dma = pltpu.SemaphoreType.DMA
    anywhere = pl.BlockSpec(memory_space=pl.ANY)
    vmem = pl.BlockSpec(memory_space=pltpu.VMEM)
    results = pl.pallas_call(
        functools.partial(kernel, (nc, nx, nh, hpd, T, R, S, D)),
        out_shape=(
            pltpu.VMEM((heads_all, R, D), bf),
            pltpu.VMEM((heads_all, T, 2 * D), bf),
            pltpu.VMEM((heads_all, EDGE, 2 * D), bf),
        ),
        in_specs=[anywhere] * 5,
        out_specs=(vmem, vmem, vmem),
        scratch_shapes=[
            pltpu.VMEM((hpd, context), jnp.int32),
            pltpu.VMEM((ny, hpd, TB), jnp.int32),
            pltpu.VMEM((ny, hpd, 2, 1, R), jnp.int32),
            pltpu.VMEM((hpd, S, TB), bf),
            pltpu.VMEM((hpd, S, LANES), bf),
            pltpu.VMEM((hpd, S, D), f32),
            pltpu.VMEM((2, ny, 2, hpd, R, D), bf),
            pltpu.VMEM((2, hpd, nh, T, D), bf),
            pltpu.VMEM((2, hpd, LANES, D), bf),
            pltpu.VMEM((ny, hpd, nx, nz, 2, S, D), bf),
            pltpu.VMEM((ny, hpd, R, D), bf),
            pltpu.VMEM((2, nc * S, R), f32),
            pltpu.VMEM((2, 2, nc * S, R), bf),
            pltpu.VMEM((ny, hpd, nx, nz, S, 2 * D), bf),
            pltpu.VMEM((plane, hpd, nz, S, 2 * D), bf),
            pltpu.VMEM((hpd, nz, S, 2 * D), bf),
            pltpu.VMEM((nz, hpd, S, 2 * D), bf),
            pltpu.VMEM((nx, nz, S, 2 * D), bf),
            pltpu.VMEM((hpd, S, 2 * D), f32),
            pltpu.VMEM((nh, hpd, T, 2 * D), bf),
            pltpu.VMEM((hpd, EDGE, 2 * D), bf),
            pltpu.SemaphoreType.REGULAR((nz,)), pltpu.SemaphoreType.REGULAR(()), dma((2 + ny,)),
            dma(()), dma((nh,)), dma(()), dma(()), dma(()), dma((ny,)), dma(()), dma((ny,)),
            dma(()), dma((nz, hpd)), dma((plane,)), dma((plane, hpd)), dma((plane,)), dma((plane, hpd)),
            dma((nx,)), dma((nx,)), dma((plane,)), dma((plane, hpd, min(3, nz))), dma(()), dma((nz, hpd)),
            dma(()), dma(()), dma(()), dma((nh,)), dma(()), dma(()),
        ],
        compiler_params=pltpu.CompilerParams(
            collective_id=0, has_side_effects=True, vmem_limit_bytes=60 << 20
        ),
    )(
        queries.reshape(heads_all, R, D), out_grad.reshape(heads_all, R, D),
        token_keys, token_values, slot_ids,
    )
    attended, grads, edges = [pltpu.with_memory_space_constraint(r, pltpu.VMEM) for r in results]
    attended, key_grad, value_grad = pl.pallas_call(
        hand_over,
        out_shape=(
            jax.ShapeDtypeStruct((heads_all, R, D), bf),
            jax.ShapeDtypeStruct((heads_all, T, D), f32),
            jax.ShapeDtypeStruct((heads_all, T, D), f32),
        ),
        in_specs=[vmem] * 3,
        out_specs=(anywhere,) * 3,
        scratch_shapes=[
            pltpu.VMEM((heads_all, T, D), f32), pltpu.VMEM((heads_all, T, D), f32), dma((3,)),
        ],
    )(attended, grads, edges)
    return attended.reshape(queries.shape), key_grad, value_grad


def solution(mesh):
    nc, nh = mesh.shape["ctx"], mesh.shape["head"]
    rows = P(None, ("ctx", "head"), None)
    grouped = P(None, ("ctx", "head"), None, None)
    return jax.shard_map(
        functools.partial(per_device, nc, nh),
        mesh=mesh,
        in_specs=(rows, rows, grouped, grouped, P("head", None)),
        out_specs=(grouped, rows, rows),
        check_vma=False,
    )
```

```python
import functools
import math

import jax
import jax.numpy as jnp
from jax import lax
from jax.experimental import pallas as pl
from jax.experimental.pallas import tpu as pltpu
from jax.sharding import PartitionSpec as P

RATIO = 4
EDGE = 16
LANES = 128
MESH = pl.DeviceIdType.MESH
neg_big = -1e30
bf, f32 = jnp.bfloat16, jnp.float32


def dot_nt(a, b):
    return lax.dot_general(a, b, (((1,), (1,)), ((), ())), preferred_element_type=f32)


def dot_tn(a, b):
    return lax.dot_general(a, b, (((0,), (0,)), ((), ())), preferred_element_type=f32)


def dot_nn(a, b):
    return lax.dot_general(a, b, (((1,), (0,)), ((), ())), preferred_element_type=f32)


def kernel(
    dims,
    q_ref, g_ref, k_ref, v_ref, id_ref,
    out_ref, rt, rx,
    idv, idb, thr, mains, edges, counts, qg, tok, ext, kv, att, raws, lows, part, red, zout, zin, straight, acc, tg, tgx,
    here, beside, loc, tok_s, tok_r, ext_s, ext_r, id_s, id_r, sw_s, sw_r,
    kz_s, kz_r, kp_s, kp_r, kd_s, kd_r, st_s, st_r, pt_s, pt_r, zs_s, zs_r, at_s, at_r, tg_s, tg_r, tx_s, tx_r,
):
    nc, nx, nh, hpd, T, R, S, D = dims
    ny, nz = nh // 2, nc // nx
    plane = nx * ny
    TB = T * nh
    NS = nc * S
    group = R // T
    scale = 1.0 / math.sqrt(D)
    ctx = lax.axis_index("ctx")
    j = lax.axis_index("head")
    y, c = j // 2, lax.rem(j, 2)
    peer = y * 2 + 1 - c
    z, x = ctx // nx, lax.rem(ctx, nx)
    spot = x * ny + y

    def remote(src, dst, ssem, rsem, to_ctx, to_head):
        return pltpu.make_async_remote_copy(
            src_ref=src, dst_ref=dst, send_sem=ssem, recv_sem=rsem,
            device_id=(to_ctx, to_head), device_id_type=MESH,
        )

    def arrived(ref, sem):
        remote(ref, ref, sem, sem, ctx, peer).wait_recv()

    def sent(ref, sem):
        remote(ref, ref, sem, sem, ctx, peer).wait_send()

    def by_layers(fn):
        for n in range(1, nz + 1):
            @pl.when(z == n - 1)
            def _():
                fn(n)

    def heads(ref, owner):
        return ref.at[pl.ds(owner * hpd, hpd)]

    last = hpd - 1
    groups = min(4, nz)

    def near_x(fn):
        @pl.loop(1, nx)
        def _(i):
            fn(lax.rem(x + i, nx), y)

    def near_y(fn):
        @pl.loop(1, ny)
        def _(i):
            fn(x, lax.rem(y + i, ny))

    def near(fn):
        near_x(fn)
        near_y(fn)

    def apart(fn):
        @pl.loop(1, nx)
        def _(i):
            @pl.loop(1, ny)
            def _(e):
                fn(lax.rem(x + i, nx), lax.rem(y + e, ny))

    def turn(to_x, to_y):
        return lax.rem(to_x - x + nx - 1, nx) * (ny - 1) + lax.rem(to_y - y + ny - 1, ny)

    def in_plane(fn):
        near(fn)
        apart(fn)

    ext[...] = jnp.zeros_like(ext)
    rx[...] = jnp.zeros_like(rx)

    get_ids = pltpu.make_async_copy(id_ref, idv, loc.at[0])
    get_ids.start()
    own_rows = []
    for yy in range(ny):
        own_rows.append(pltpu.make_async_copy(heads(q_ref, yy * 2 + c), qg.at[0, yy, 0], loc.at[1 + yy]))
        own_rows.append(pltpu.make_async_copy(heads(g_ref, yy * 2 + c), qg.at[0, yy, 1], loc.at[1 + yy]))

    barrier = pltpu.get_barrier_semaphore()

    def greet(to_ctx, to_head):
        pl.semaphore_signal(barrier, inc=1, device_id=(to_ctx, to_head), device_id_type=MESH)

    @pl.loop(1, nh)
    def _(i):
        greet(ctx, lax.rem(j + i, nh))

    @pl.loop(x + 1, nx)
    def _(to_x):
        @pl.loop(0, ny)
        def _(yy):
            greet(z * nx + to_x, yy * 2 + c)

    @pl.loop(z + 1, nz)
    def _(to):
        greet(to * nx + x, j)

    @pl.when(ctx < nc - 1)
    def _():
        greet(ctx + 1, 0)

    for cp in own_rows:
        cp.start()

    follows = (j == 0) & (ctx > 0)
    pl.semaphore_wait(barrier, nh - 1 + x * ny + z + jnp.where(follows, nh, 0))

    @pl.loop(0, z)
    def _(to):
        pl.semaphore_signal(here.at[z], inc=1, device_id=(to * nx + x, j), device_id_type=MESH)

    @pl.loop(0, x)
    def _(to_x):
        @pl.loop(0, ny)
        def _(yy):
            pl.semaphore_signal(beside, inc=1, device_id=(z * nx + to_x, yy * 2 + c), device_id_type=MESH)

    own_tok = [
        pltpu.make_async_copy(heads(k_ref, j), tok.at[0, :, j], loc.at[1 + ny]),
        pltpu.make_async_copy(heads(v_ref, j), tok.at[1, :, j], loc.at[1 + ny]),
    ]
    for cp in own_tok:
        cp.start()

    @pl.loop(1, nh)
    def _(i):
        to = lax.rem(j + i, nh)
        remote(heads(k_ref, to), tok.at[0, :, j], tok_s, tok_r, ctx, to).start()
        remote(heads(v_ref, to), tok.at[1, :, j], tok_s, tok_r, ctx, to).start()

    @pl.when(follows)
    def _():
        @pl.loop(0, nh)
        def _(to):
            for which, src in ((0, k_ref), (1, v_ref)):
                remote(
                    src.at[pl.ds(to * hpd, hpd), pl.ds(0, EDGE)], ext.at[which, :, pl.ds(0, EDGE)],
                    ext_s, ext_r, ctx - 1, to,
                ).start()

    get_ids.wait()
    idb[y] = idv[:, pl.ds(pl.multiple_of(ctx * TB, LANES), TB)] - ctx * S

    @pl.loop(1, ny)
    def _(i):
        remote(idb.at[y], idb.at[y], id_s, id_r.at[y], ctx, lax.rem(y + i, ny) * 2 + c).start()

    @pl.loop(0, ny)
    def _(i):
        yy = lax.rem(y + i, ny)
        remote(heads(q_ref, yy * 2 + 1 - c), qg.at[1, yy, 0], sw_s, sw_r.at[yy], ctx, peer).start()
        remote(heads(g_ref, yy * 2 + 1 - c), qg.at[1, yy, 1], sw_s, sw_r.at[yy], ctx, peer).start()

    next_at = pl.multiple_of(jnp.minimum(ctx + 1, nc - 1) * TB, LANES)

    for h in range(hpd):
        main_ids = idv[h:h + 1, pl.ds(pl.multiple_of(ctx * TB, LANES), TB)] - ctx * S
        edge_ids = jnp.where(ctx < nc - 1, idv[h:h + 1, pl.ds(next_at, LANES)] - ctx * S, -1)
        main = (lax.broadcasted_iota(jnp.int32, (S, TB), 0) == main_ids).astype(f32)
        edge = (lax.broadcasted_iota(jnp.int32, (S, LANES), 0) == edge_ids).astype(f32)
        count = jnp.sum(main, axis=1, keepdims=True) + jnp.sum(edge, axis=1, keepdims=True)
        mains[h], edges[h] = main.astype(bf), edge.astype(bf)
        counts[h] = jnp.broadcast_to(count, (S, D))

    arrived(tok.at[:, :, pl.ds(0, nh - 1)], tok_r)
    own = tok.at[:, :, j]
    pltpu.make_async_copy(own, own, loc.at[1 + ny]).wait()

    @pl.when(ctx < nc - 1)
    def _():
        arrived(ext.at[:, :, pl.ds(0, EDGE)], ext_r)

    for h in range(hpd):
        for which in range(2):
            total = dot_nn(mains[h], tok[which, h].reshape(TB, D)) + dot_nn(edges[h], ext[which, h])
            kv[y, h, x, z, which] = (total / counts[h]).astype(bf)

    def spread(h, zs):
        blk = kv.at[y, h, x, zs]

        def give(sems, to_x, to_y):
            to = to_x * ny + to_y
            remote(blk, blk, sems.at[to], kp_r.at[spot, h], z * nx + to_x, to_y * 2 + c).start()

        near(functools.partial(give, kp_s))
        if zs is z:
            apart(functools.partial(give, kp_s))

    @pl.when(x < nx - 1)
    def _():
        pl.semaphore_wait(beside, (nx - 1 - x) * ny)

    @pl.loop(z + 1, nz)
    def _(i):
        to = nz + z - i
        pl.semaphore_wait(here.at[to], 1)
        for h in range(hpd):
            blk = kv.at[y, h, x, z]
            remote(blk, blk, kz_s, kz_r.at[z, h], to * nx + x, j).start()

    for h in range(hpd):
        spread(h, z)

    for h in range(hpd):
        def lift(frm_x, frm_y):
            frm = frm_x * ny + frm_y
            blk = kv.at[frm_y, h, frm_x, z]
            way = turn(frm_x, frm_y)
            arrived(blk, kp_r.at[frm, h])

            @pl.loop(z + 1, nz)
            def _(i):
                to = nz + z - i
                remote(blk, blk, kd_s.at[way], kd_r.at[way, h], to * nx + x, j).start()

        apart(lift)

        @pl.loop(0, z)
        def _(i):
            zs = z - 1 - i
            arrived(kv.at[y, h, x, zs], kz_r.at[zs, h])
            spread(h, zs)

    @pl.loop(1, ny)
    def _(i):
        yy = lax.rem(y + i, ny)
        arrived(idb.at[yy], id_r.at[yy])

    for t in range(2):
        core = c if t == 0 else 1 - c
        token = lax.broadcasted_iota(jnp.int32, (TB, R), 0) - (y * 2 + core) * T
        first = lax.broadcasted_iota(jnp.int32, (TB, R), 1) - token * group
        pick = ((first >= 0) & (first < group)).astype(f32).astype(bf)
        for yy in range(ny):
            for h in range(hpd):
                ids = idb[yy, h:h + 1].astype(f32).astype(bf)
                row = dot_nn(jnp.broadcast_to(ids, (16, TB)), pick)
                thr[yy, h, t] = row[:1].astype(jnp.int32)

    def total(h, zb, g):
        out = part[y, h, x, zb].astype(f32)
        for i in range(nx):
            for e in range(ny):
                if i + e > 0 and (h < last or g > 0 or e > 0):
                    out += red[lax.rem(x + i, nx) * ny + lax.rem(y + e, ny), h, zb].astype(f32)
        return out

    def givers(h, g, fn):
        near_y(fn)
        apart(fn)
        if h < last or g > 0:
            near_x(fn)

    def pass_on(h, zb, g):
        zout[h, zb] = total(h, zb, g).astype(bf)
        remote(zout.at[h, zb], zin.at[h, z], zs_s, zs_r.at[h], zb * nx + x, j).start()

    def group_of(g, n):
        first = min(g, n)
        return pl.ds(first, (n if g == groups - 1 else min(g + 1, n)) - first)

    def give(h, yy, xs, g):
        def send(layers):
            remote(
                part.at[yy, h, xs, layers], red.at[spot, h, layers],
                pt_s.at[jnp.where((h == last) & (yy == y), spot, xs * ny + yy)], pt_r.at[spot, h, g],
                z * nx + xs, yy * 2 + c,
            ).start()

        by_layers(lambda n: n > g and send(group_of(g, n)))

    def give_all(h, yy, own, g):
        @pl.loop(own, nx)
        def _(i):
            give(h, yy, lax.rem(x + i, nx), g)

    def give_straight(to_x, to_y):
        remote(part.at[y, last, to_x, 0], straight.at[x, z], st_s.at[to_x], st_r.at[x], to_x, j).start()

    def sum_plane():
        for g in range(groups):
            for h in range(hpd):
                givers(h, g, lambda fx, fy: by_layers(lambda n: n > g and arrived(
                    red.at[fx * ny + fy, h, group_of(g, n)], pt_r.at[fx * ny + fy, h, g]
                )))

                @pl.loop(g, jnp.minimum(z, nz if g == groups - 1 else g + 1))
                def _(zb):
                    pass_on(h, zb, g)

                @pl.when((z == g) | ((z > g) & (g == groups - 1)))
                def _():
                    acc[h] = total(h, z, g)

    def attend(yy, h, n):
        width, step = nx * n * S, 2 * S
        keys = kv[yy, h, :, :n, 0].reshape(width, D)
        vals = kv[yy, h, :, :n, 1].reshape(width, D)
        chunks = [slice(at, at + step) for at in range(0, width, step)]
        slot = lax.broadcasted_iota(jnp.int32, (S, R), 0)

        def score(t):
            top = None
            for at in chunks:
                scores = dot_nt(keys[at], qg[t, yy, 0, h])
                for half in range(2):
                    xb, zb = divmod(at.start // S + half, n)
                    part_scores = scores[half * S:(half + 1) * S]
                    if zb == n - 1:
                        bar = thr[yy, h, t] - (zb * nx + xb - ctx) * S
                        part_scores = jnp.where(slot <= bar, part_scores, neg_big)
                    begin = at.start + half * S
                    raws[t, begin:begin + S] = part_scores
                    high = jnp.max(part_scores, axis=0, keepdims=True)
                    top = high if top is None else jnp.maximum(top, high)
            return top

        def power(t, top):
            whole = None
            for at in chunks:
                raw = jnp.exp2((raws[t, at] - top) * (scale * math.log2(math.e)))
                raws[t, at] = raw
                some = jnp.sum(raw, axis=0, keepdims=True)
                whole = some if whole is None else whole + some
            return 1.0 / whole

        def look(t, inverse):
            for at in chunks:
                lows[t, 0, at] = (raws[t, at] * inverse).astype(bf)
            seen = dot_tn(vals, lows[t, 0, :width]).astype(bf)
            if t == 0:
                out_ref[(yy * 2 + c) * hpd + h] = seen.T
            else:
                att[yy, h] = seen.T
            return jnp.sum(qg[t, yy, 1, h].T.astype(f32) * seen.astype(f32), axis=0, keepdims=True)

        def slopes(t, inverse, row_dot):
            rows, grads = qg[t, yy, 0, h], qg[t, yy, 1, h]
            for at in chunks:
                lows[t, 1, at] = ((raws[t, at] * inverse) * (dot_nt(vals[at], grads) - row_dot)).astype(bf)
            return dot_nn(lows[t, 1, :width], rows), dot_nn(lows[t, 0, :width], grads)

        tops = [score(t) for t in range(2)]
        inverses = [power(t, tops[t]) for t in range(2)]
        row_dots = [look(t, inverses[t]) for t in range(2)]
        grads = [slopes(t, inverses[t], row_dots[t]) for t in range(2)]
        part[yy, h, :, :n, :, :D] = ((grads[0][0] + grads[1][0]) * scale).astype(bf).reshape(nx, n, S, D)
        part[yy, h, :, :n, :, D:] = (grads[0][1] + grads[1][1]).astype(bf).reshape(nx, n, S, D)

    @pl.loop(0, hpd * ny)
    def _(u):
        h = u // ny
        k = lax.rem(u + jnp.where(h == last, 1, 0), ny)
        yy = lax.rem(y + k, ny)

        @pl.when(h == 0)
        def _():
            pltpu.make_async_copy(qg.at[0, yy], qg.at[0, yy], loc.at[1 + yy]).wait()
            arrived(qg.at[1, yy], sw_r.at[yy])

        @pl.loop(0, nx)
        def _(i):
            xs = lax.rem(x + i, nx)

            @pl.when((i > 0) | (k > 0))
            def _():
                @pl.when((i == 0) | (k == 0))
                def _():
                    by_layers(lambda n: arrived(kv.at[yy, h, xs, pl.ds(0, n)], kp_r.at[xs * ny + yy, h]))

                @pl.when((i > 0) & (k > 0))
                def _():
                    by_layers(lambda n: n > 1 and arrived(
                        kv.at[yy, h, xs, pl.ds(0, n - 1)], kd_r.at[turn(xs, yy), h]
                    ))

        by_layers(lambda n: attend(yy, h, n))

        @pl.when((k == 0) & (h == last))
        def _():
            near_x(give_straight)
            for g in range(1, groups):
                give_all(h, yy, 1, g)

        @pl.when((k > 0) | (h < last))
        def _():
            own = jnp.where(k == 0, 1, 0)
            give_all(h, yy, own, 0)

            @pl.when((h < last) & (k < ny - 1))
            def _():
                for g in range(1, groups):
                    give_all(h, yy, own, g)

            @pl.when((h == last) & (k == ny - 1))
            def _():
                for g in range(1, groups):
                    for hh in range(hpd):
                        @pl.loop(1, ny)
                        def _(e):
                            @pl.when((hh == last) | (e == ny - 1))
                            def _():
                                give_all(hh, lax.rem(y + e, ny), 0, g)

        remote(att.at[yy, h], out_ref.at[(yy * 2 + c) * hpd + h], at_s, at_r, ctx, peer).start()

    sum_plane()

    for h in range(hpd):
        by_layers(lambda n: n < nz and arrived(zin.at[h, pl.ds(n, nz - n)], zs_r.at[h]))

        @pl.loop(z + 1, nz)
        def _(frm):
            acc[h] += zin[h, frm].astype(f32)

        if h == last:
            @pl.when(z == 0)
            def _():
                def add(frm_x, frm_y):
                    arrived(straight.at[frm_x], st_r.at[frm_x])
                    acc[h] += sum(straight[frm_x, zb].astype(f32) for zb in range(nz))

                near_x(add)

        mean = acc[h].astype(bf).astype(f32)
        twice = jnp.concatenate([counts[h], counts[h]], axis=1)
        unit = (mean / twice).astype(bf)
        spread_rows = dot_tn(mains[h], unit).astype(bf)
        for to in range(nh):
            tg[to, h] = spread_rows[to * T:(to + 1) * T]

        @pl.loop(1, nh)
        def _(i):
            to = lax.rem(j + i, nh)
            remote(tg.at[to, h], rt.at[j * hpd + h], tg_s, tg_r, ctx, to).start()

        tgx[h] = dot_tn(edges[h], unit)[:EDGE].astype(bf)

    @pl.when(ctx < nc - 1)
    def _():
        remote(tgx, heads(rx, j), tx_s, tx_r, ctx + 1, 0).start()

    rt[pl.ds(j * hpd, hpd)] = tg[j]

    sent(tok.at[:, :, pl.ds(0, nh - 1)], tok_s)

    @pl.when(follows)
    def _():
        sent(tok.at[:, :, :, pl.ds(0, EDGE)], ext_s)

    sent(idb.at[pl.ds(0, ny - 1)], id_s)
    sent(qg.at[1], sw_s)
    sent(att, at_s)
    arrived(att, at_r)
    for n in range(1, nz):
        @pl.when(z == nz - 1 - n)
        def _():
            sent(kv.at[y, :, x, pl.ds(0, n)], kz_s)
            apart(lambda fx, fy: sent(kv.at[fy, :, fx, pl.ds(0, n)], kd_s.at[turn(fx, fy)]))

        @pl.when(z == n)
        def _():
            sent(zout.at[:, pl.ds(0, n)], zs_s)

    def near_sent(to_x, to_y):
        to = to_x * ny + to_y
        by_layers(lambda n: sent(kv.at[y, :, x, pl.ds(0, n)], kp_s.at[to]))

    def parts_sent(to_x, to_y, count):
        by_layers(lambda n: sent(part.at[to_y, pl.ds(0, count), to_x, pl.ds(0, n)], pt_s.at[to_x * ny + to_y]))

    near_y(lambda tx, ty: parts_sent(tx, ty, hpd))
    if hpd > 1:
        near_x(lambda tx, ty: parts_sent(tx, ty, hpd - 1))

    apart(lambda tx, ty: parts_sent(tx, ty, hpd))
    near_x(lambda tx, ty: sent(part.at[y, last, tx, 0], st_s.at[tx]))
    by_layers(lambda n: n > 1 and sent(
        part.at[y, last, pl.ds(0, nx - 1), pl.ds(1, n - 1)], pt_s.at[spot]
    ))

    def apart_sent(to_x, to_y):
        sent(kv.at[y, :, x, 0], kp_s.at[to_x * ny + to_y])

    near(near_sent)
    apart(apart_sent)

    arrived(rt.at[pl.ds(0, (nh - 1) * hpd)], tg_r)

    @pl.when(follows)
    def _():
        arrived(rx, tx_r)

    sent(tg.at[pl.ds(0, nh - 1)], tg_s)

    @pl.when(ctx < nc - 1)
    def _():
        sent(tgx, tx_s)


def hand_over(a_ref, t_ref, x_ref, a_out, k_out, v_out, kbuf, vbuf, sem):
    D = k_out.shape[-1]
    whole = pltpu.make_async_copy(a_ref, a_out, sem.at[0])
    whole.start()
    copies = [whole]
    for i, (buf, out) in enumerate(((kbuf, k_out), (vbuf, v_out))):
        cols = slice(i * D, (i + 1) * D)
        buf[...] = t_ref[:, :, cols].astype(f32)
        buf[:, :EDGE] += x_ref[:, :, cols].astype(f32)
        copies.append(pltpu.make_async_copy(buf, out, sem.at[1 + i]))
        copies[-1].start()
    for cp in copies:
        cp.wait()


def per_device(nc, nh, token_keys, token_values, queries, out_grad, slot_ids):
    heads_all, T, D = token_keys.shape
    group = queries.shape[2]
    hpd, context = slot_ids.shape
    R = queries.shape[1] * group
    TB = T * nh
    S = TB // RATIO
    ny = nh // 2
    nx = 2 ** ((nc.bit_length() - 1) // 2)
    nz = nc // nx
    plane, ways = nx * ny, (nx - 1) * (ny - 1)
    dma = pltpu.SemaphoreType.DMA
    anywhere = pl.BlockSpec(memory_space=pl.ANY)
    vmem = pl.BlockSpec(memory_space=pltpu.VMEM)
    results = pl.pallas_call(
        functools.partial(kernel, (nc, nx, nh, hpd, T, R, S, D)),
        out_shape=(
            pltpu.VMEM((heads_all, R, D), bf),
            pltpu.VMEM((heads_all, T, 2 * D), bf),
            pltpu.VMEM((heads_all, EDGE, 2 * D), bf),
        ),
        in_specs=[anywhere] * 5,
        out_specs=(vmem, vmem, vmem),
        scratch_shapes=[
            pltpu.VMEM((hpd, context), jnp.int32),
            pltpu.VMEM((ny, hpd, TB), jnp.int32),
            pltpu.VMEM((ny, hpd, 2, 1, R), jnp.int32),
            pltpu.VMEM((hpd, S, TB), bf),
            pltpu.VMEM((hpd, S, LANES), bf),
            pltpu.VMEM((hpd, S, D), f32),
            pltpu.VMEM((2, ny, 2, hpd, R, D), bf),
            pltpu.VMEM((2, hpd, nh, T, D), bf),
            pltpu.VMEM((2, hpd, LANES, D), bf),
            pltpu.VMEM((ny, hpd, nx, nz, 2, S, D), bf),
            pltpu.VMEM((ny, hpd, R, D), bf),
            pltpu.VMEM((2, nc * S, R), f32),
            pltpu.VMEM((2, 2, nc * S, R), bf),
            pltpu.VMEM((ny, hpd, nx, nz, S, 2 * D), bf),
            pltpu.VMEM((plane, hpd, nz, S, 2 * D), bf),
            pltpu.VMEM((hpd, nz, S, 2 * D), bf),
            pltpu.VMEM((hpd, nz, S, 2 * D), bf),
            pltpu.VMEM((nx, nz, S, 2 * D), bf),
            pltpu.VMEM((hpd, S, 2 * D), f32),
            pltpu.VMEM((nh, hpd, T, 2 * D), bf),
            pltpu.VMEM((hpd, EDGE, 2 * D), bf),
            pltpu.SemaphoreType.REGULAR((nz,)), pltpu.SemaphoreType.REGULAR(()), dma((2 + ny,)),
            dma(()), dma(()), dma(()), dma(()), dma(()), dma((ny,)), dma(()), dma((ny,)),
            dma(()), dma((nz, hpd)), dma((plane,)), dma((plane, hpd)), dma((ways,)), dma((ways, hpd)),
            dma((nx,)), dma((nx,)), dma((plane,)), dma((plane, hpd, min(4, nz))), dma(()), dma((hpd,)),
            dma(()), dma(()), dma(()), dma(()), dma(()), dma(()),
        ],
        compiler_params=pltpu.CompilerParams(
            collective_id=0, has_side_effects=True, vmem_limit_bytes=60 << 20
        ),
    )(
        queries.reshape(heads_all, R, D), out_grad.reshape(heads_all, R, D),
        token_keys, token_values, slot_ids,
    )
    attended, grads, edges = [pltpu.with_memory_space_constraint(r, pltpu.VMEM) for r in results]
    attended, key_grad, value_grad = pl.pallas_call(
        hand_over,
        out_shape=(
            jax.ShapeDtypeStruct((heads_all, R, D), bf),
            jax.ShapeDtypeStruct((heads_all, T, D), f32),
            jax.ShapeDtypeStruct((heads_all, T, D), f32),
        ),
        in_specs=[vmem] * 3,
        out_specs=(anywhere,) * 3,
        scratch_shapes=[
            pltpu.VMEM((heads_all, T, D), f32), pltpu.VMEM((heads_all, T, D), f32), dma((3,)),
        ],
    )(attended, grads, edges)
    return attended.reshape(queries.shape), key_grad, value_grad


def solution(mesh):
    nc, nh = mesh.shape["ctx"], mesh.shape["head"]
    rows = P(None, ("ctx", "head"), None)
    grouped = P(None, ("ctx", "head"), None, None)
    return jax.shard_map(
        functools.partial(per_device, nc, nh),
        mesh=mesh,
        in_specs=(rows, rows, grouped, grouped, P("head", None)),
        out_specs=(grouped, rows, rows),
        check_vma=False,
    )
```
